512 devices in a mesh: expert: 128 (over z, y, core), dp: 4 (over x).
Axes of the slice: x: 4, y: 8, z: 8, core: 2. Of those that a mesh axis runs over, the one named last changes fastest.
Arguments:
- hidden_in: bfloat16 [4, 16384, 2048], P('dp', 'expert'), may hold values from -6 to 6
- out_grad: bfloat16 [4, 16384, 2048], P('dp', 'expert'), may hold values from -6 to 6
- routes: int32 [4, 16384, 2], P('dp', 'expert'), may hold values from 0 to 127, all different within a row; in each aligned block of 128 rows (0 to 127, 128 to 255, ..., all dimensions but the last counted through in order) at most 3 rows name the same one
- gate_num: int32 [4, 16384, 2], P('dp', 'expert'), may hold values from 64 to 1023
- doc_lengths: int32 [4, 32], P('dp'), may hold values from 1 to 8192, 16384 in all within a row
- w_gate: bfloat16 [128, 768, 2048], P('expert', 'dp'), may hold values from -0.125 to 0.125
- w_up: bfloat16 [128, 768, 2048], P('expert', 'dp'), may hold values from -0.125 to 0.125
- w_down: bfloat16 [128, 768, 2048], P('expert', 'dp'), may hold values from -0.21875 to 0.21875
- a_gate: bfloat16 [128, 2048, 16], P('expert'), may hold values from -0.125 to 0.125
- b_gate: bfloat16 [128, 16, 768], P('expert'), may hold values from -0.59765625 to 0.59765625
- a_up: bfloat16 [128, 2048, 16], P('expert'), may hold values from -0.125 to 0.125
- b_up: bfloat16 [128, 16, 768], P('expert'), may hold values from -0.59765625 to 0.59765625
- a_down: bfloat16 [128, 768, 16], P('expert'), may hold values from -0.21875 to 0.21875
- b_down: bfloat16 [128, 16, 2048], P('expert'), may hold values from -0.59765625 to 0.59765625
Outputs:
- input_grad: bfloat16 [4, 16384, 2048], P('dp', 'expert')
- grad_a_gate: float32 [128, 2048, 16], P('expert', 'dp')
- grad_b_gate: float32 [128, 16, 768], P('expert', None, 'dp')
- grad_a_up: float32 [128, 2048, 16], P('expert', 'dp')
- grad_b_up: float32 [128, 16, 768], P('expert', None, 'dp')
- grad_a_down: float32 [128, 768, 16], P('expert', 'dp')
- grad_b_down: float32 [128, 16, 2048], P('expert', None, 'dp')
The draws below stay inside these ranges and needn't reach their ends.
Inputs may be any that keep to these rules, and one draw needn't show every extreme that they name: `routes`: each row names 2 different experts; the rows of one device name one expert 3 times at most. `doc_lengths`: each row sums to 16384.
All inputs are finite; a program needn't handle non-finite values.
Results may differ from the reference program's by a relative error of at most 0.0074.
Values may be sent and summed in bfloat16 or wider, within the bound.
No kernel may reach another device: no remote copies, remote signals or barrier semaphores. Data moves between devices by JAX's collectives and lax.ppermute only.
A program may use at most 64 MiB of HBM per device.

```python
import math
from functools import partial
import jax
import jax.numpy as jnp
import numpy as np
from jax import lax

D = 2048
FF = 768
RANK = 16
TOPK = 2
TOK_DEV = 128
EXPERTS = 128
GROUP_TOK = 16384
CAP = 3
DOCS = 32
MAXDOC = 8192
N_EXPERT = 128
N_DP = 4


def place_ends(array, rng, least, top_value):
    longest = array.shape.index(max(array.shape))
    spots = []
    for shift in (0, 1):
        where = [jax.random.randint(jax.random.fold_in(rng, axis), (), 0, length) for axis, length in enumerate(array.shape)]
        where[longest] = (where[longest] + shift) % array.shape[longest]
        spots.append(tuple(where))
    return array.at[spots[0]].set(least).at[spots[1]].set(top_value)


def block_levels(own_key, extent, cuts, smallest, largest):
    def one(dim, blocks):
        heights = jax.random.uniform(jax.random.fold_in(jax.random.fold_in(own_key, 6), dim), (blocks,), jnp.float32, smallest / len(cuts), largest / len(cuts))
        return jnp.repeat(jnp.exp(heights), extent[dim] // blocks).reshape((-1,) + (1,) * (len(extent) - dim - 1))

    factor_of = one(*cuts[0])
    for cut in cuts[1:]:
        factor_of = factor_of * one(*cut)
    return factor_of


def split_up(count, total, most, skew):
    portions = [(1 << 20) // math.isqrt(standing ** skew) + 1 for standing in range(2, count + 1)]
    surplus, counts = total - most - (count - 1), [1] * (count - 1)
    while surplus > 0:
        movable = [i for i in range(count - 1) if counts[i] < most]
        mass, left = sum([portions[i] for i in movable]), surplus
        for i in movable:
            extra = min(most - counts[i], max(1, left * portions[i] // mass), surplus)
            counts[i] = counts[i] + extra
            surplus = surplus - extra
    return np.array([most] + counts)


def ragged(key, number_of, total, bound, skew):
    if number_of == 2:
        one = jax.random.randint(key, (), max(1, total - bound), min(bound, total - 1) + 1)
        return jnp.stack([one, total - one])
    sizes = jnp.asarray(split_up(number_of, total, bound, skew), jnp.int32)
    pairs = (number_of - 1) // 2
    donor, sink = sizes[1:1 + 2 * pairs:2], sizes[2:2 + 2 * pairs:2]
    room = jnp.minimum(donor - 1, bound - sink)
    moved = jax.random.randint(jax.random.fold_in(key, 1), (pairs,), 0, 1 << 20) % (room + 1)
    sizes = sizes.at[1:1 + 2 * pairs:2].set(donor - moved).at[2:2 + 2 * pairs:2].set(sink + moved)
    return sizes[jax.random.permutation(jax.random.fold_in(key, 2), number_of)]


def deal_out(stream_key, own, number, rows, amount, top, bound, lean):
    ranking = jax.random.permutation(stream_key, amount)
    crowded, usual = load_shares(amount, rows * top, bound, lean, True), load_shares(amount, rows * top, bound, lean, False)
    places = jnp.arange(amount)

    def named(tallies, turn):
        used = int((tallies > 0).sum())
        fixed = max(1, used // 4)
        shifted = fixed + (places - fixed + turn * (used - fixed)) % max(1, amount - fixed)
        return jnp.zeros((amount,), jnp.int32).at[ranking[jnp.where(places < fixed, places, shifted)]].set(jnp.asarray(tallies, jnp.int32))

    tallies = jnp.where(number % 4 == 0, named(crowded, number // 4), named(usual, number - number // 4 - 1))
    mixed = jax.random.permutation(jax.random.fold_in(own, 3), amount)
    source_of, taker = mixed[0:amount // 2 * 2:2], mixed[1:amount // 2 * 2:2]
    room = jnp.minimum(tallies[source_of] - 1, bound - tallies[taker]) // 2
    room = jnp.where((source_of == ranking[0]) | (taker == ranking[0]) | (tallies[taker] == 0), 0, jnp.maximum(room, 0))
    shifted = jax.random.randint(jax.random.fold_in(own, 4), (amount // 2,), 0, 1 << 20) % (room + 1)
    tallies = tallies.at[source_of].add(-shifted).at[taker].add(shifted)
    members = jnp.searchsorted(jnp.cumsum(tallies), jnp.arange(rows * top), side="right").astype(jnp.int32)
    grid = members.reshape(top, rows).T
    grid = grid[jax.random.permutation(jax.random.fold_in(own, 1), rows)]
    turn = jax.random.randint(jax.random.fold_in(own, 2), (rows, 1), 0, top)
    return jnp.take_along_axis(grid, (jnp.arange(top)[None, :] + turn) % top, axis=1)


def load_shares(number_of, total, bound, lean, full):
    portions = [(1 << 20) // math.isqrt(grade ** lean) + 1 for grade in range(1, number_of + 1)]
    largest = bound if full else min(bound, max(-(-total // number_of), total * portions[0] // sum(portions)))
    least = 1 if total - largest >= number_of - 1 else 0
    counts, surplus = [largest] + [least] * (number_of - 1), total - largest - least * (number_of - 1)
    while surplus > 0:
        free = [i for i in range(1, number_of) if counts[i] < largest] or [i for i in range(1, number_of) if counts[i] < bound]
        mass, remaining = sum([portions[i] for i in free]), surplus
        for i in free:
            more = min(bound - counts[i], max(1, remaining * portions[i] // mass), surplus)
            counts[i] = counts[i] + more
            surplus = surplus - more
    return np.array(counts)


def gaussian(rng, extent, spread, most, pieces=(), kind=jnp.bfloat16):
    values = jax.random.normal(rng, extent, jnp.float32) * spread
    if len(pieces) > 0:
        values = block_levels(rng, extent, pieces, -0.22, 0.18) * values
    return jnp.clip(values, min=-most, max=most).astype(kind)


def setup_inputs(seed: int = 0) -> dict:
    key_list = jax.random.split(jax.random.key(seed), 15)
    hidden_in = gaussian(key_list[0], (N_DP, GROUP_TOK, D), 1.0, 6.0, ((0, 4), (1, 128)))
    out_grad = gaussian(key_list[1], (N_DP, GROUP_TOK, D), 1.0, 6.0, ((0, 4), (1, 128)))
    routes_keys = jax.random.split(jax.random.fold_in(key_list[2], 1), N_DP * GROUP_TOK // TOK_DEV)
    routes_turns = jax.random.permutation(jax.random.fold_in(key_list[2], 3), N_DP * GROUP_TOK // TOK_DEV)
    routes = jax.vmap(lambda own, number: deal_out(jax.random.fold_in(key_list[2], 2), own, number, TOK_DEV, EXPERTS, TOPK, CAP, 2))(routes_keys, routes_turns).reshape((N_DP, GROUP_TOK, TOPK))
    gate_num = place_ends(jax.random.randint(key_list[3], (N_DP, GROUP_TOK, TOPK), 64, 1024), jax.random.fold_in(key_list[3], 1), 64, 1023).astype(jnp.int32)
    doc_lengths = jax.vmap(lambda own: ragged(own, DOCS, GROUP_TOK, MAXDOC, 2))(jax.random.split(key_list[4], N_DP)).reshape((N_DP, DOCS)).astype(jnp.int32)
    w_gate = gaussian(key_list[5], (EXPERTS, FF, D), D ** -0.5, 0.125, ((0, 128), (1, 4)))
    w_up = gaussian(key_list[6], (EXPERTS, FF, D), D ** -0.5, 0.125, ((0, 128), (1, 4)))
    w_down = gaussian(key_list[7], (EXPERTS, FF, D), FF ** -0.5, 0.21875, ((0, 128), (1, 4)))
    a_gate = gaussian(key_list[8], (EXPERTS, D, RANK), D ** -0.5, 0.125, ((0, 128),))
    b_gate = gaussian(key_list[9], (EXPERTS, RANK, FF), 0.1, 0.59765625, ((0, 128),))
    a_up = gaussian(key_list[10], (EXPERTS, D, RANK), D ** -0.5, 0.125, ((0, 128),))
    b_up = gaussian(key_list[11], (EXPERTS, RANK, FF), 0.1, 0.59765625, ((0, 128),))
    a_down = gaussian(key_list[12], (EXPERTS, FF, RANK), FF ** -0.5, 0.21875, ((0, 128),))
    b_down = gaussian(key_list[13], (EXPERTS, RANK, D), 0.1, 0.59765625, ((0, 128),))
    return {"hidden_in": hidden_in, "out_grad": out_grad, "routes": routes, "gate_num": gate_num, "doc_lengths": doc_lengths, "w_gate": w_gate, "w_up": w_up, "w_down": w_down, "a_gate": a_gate, "b_gate": b_gate, "a_up": a_up, "b_up": b_up, "a_down": a_down, "b_down": b_down}


ADAPTER_SCALE = 2.0

def simple_matmul(left, right):
    return jnp.dot(left, right, preferred_element_type=jnp.float32)

def contract_trailing(left, right):
    return lax.dot_general(left, right, (((1,), (1,)), ((), ())), preferred_element_type=jnp.float32)

def contract_leading(left, right):
    return lax.dot_general(left, right, (((0,), (0,)), ((), ())), preferred_element_type=jnp.float32)

def row_factor(position, lengths, numerators, group_tokens, doc_count):
    ends = jnp.cumsum(lengths).astype(jnp.int32)
    starts = ends - lengths
    inside = (position[:, None] >= starts[None, :]) & (position[:, None] < ends[None, :])
    own_length = lax.optimization_barrier(jnp.sum(jnp.where(inside, lengths[None, :], 0), axis=1)).astype(jnp.int32)
    weight = jnp.sqrt(jnp.float32(group_tokens) / (doc_count * own_length).astype(jnp.float32))
    return numerators.astype(jnp.float32) / 1024.0 * weight[:, None]

def expert_rows(dispatched_rows, gradient_row_block, gate_weight, up_weight, down_weight, gate_adapter_left, gate_adapter_right, up_adapter_left, up_adapter_right, down_adapter_left, bdown):
    gate_rank_rows = simple_matmul(dispatched_rows, gate_adapter_left).astype(jnp.bfloat16)
    up_rank_rows = simple_matmul(dispatched_rows, up_adapter_left).astype(jnp.bfloat16)
    rank_space_gradient = contract_trailing(gradient_row_block, bdown).astype(jnp.bfloat16)
    gate_activation = contract_trailing(dispatched_rows, gate_weight) + ADAPTER_SCALE * simple_matmul(gate_rank_rows, gate_adapter_right)
    upward_projection = contract_trailing(dispatched_rows, up_weight) + ADAPTER_SCALE * simple_matmul(up_rank_rows, up_adapter_right)
    hidden_activation_gradient = contract_trailing(gradient_row_block, down_weight) + ADAPTER_SCALE * contract_trailing(rank_space_gradient, down_adapter_left)
    sigma = jax.nn.sigmoid(gate_activation)
    active = gate_activation * sigma
    hidden_activation = (active * upward_projection).astype(jnp.bfloat16)
    gate_branch_gradient = (hidden_activation_gradient * upward_projection * sigma * (1.0 + gate_activation * (1.0 - sigma))).astype(jnp.bfloat16)
    up_branch_gradient = (hidden_activation_gradient * active).astype(jnp.bfloat16)
    gate_rank_gradient = contract_trailing(gate_branch_gradient, gate_adapter_right).astype(jnp.bfloat16)
    up_rank_gradient = contract_trailing(up_branch_gradient, up_adapter_right).astype(jnp.bfloat16)
    down_rank_rows = simple_matmul(hidden_activation, down_adapter_left).astype(jnp.bfloat16)
    per_row_gradient = (simple_matmul(gate_branch_gradient, gate_weight) + simple_matmul(up_branch_gradient, up_weight) + ADAPTER_SCALE * (contract_trailing(gate_rank_gradient, gate_adapter_left) + contract_trailing(up_rank_gradient, up_adapter_left))).astype(jnp.bfloat16)
    gradient_tuple = (ADAPTER_SCALE * contract_leading(dispatched_rows, gate_rank_gradient), ADAPTER_SCALE * contract_leading(gate_rank_rows, gate_branch_gradient), ADAPTER_SCALE * contract_leading(dispatched_rows, up_rank_gradient), ADAPTER_SCALE * contract_leading(up_rank_rows, up_branch_gradient), ADAPTER_SCALE * contract_leading(hidden_activation, rank_space_gradient), ADAPTER_SCALE * contract_leading(down_rank_rows, gradient_row_block))
    return (per_row_gradient, gradient_tuple)

def reference(hidden_in, out_grad, routes, gate_num, doc_lengths, w_gate, w_up, w_down, a_gate, b_gate, a_up, b_up, a_down, b_down):
    position = jnp.arange(GROUP_TOK, dtype=jnp.int32)
    factor = jax.vmap(partial(row_factor, position), in_axes=(0, 0, None, None))(doc_lengths, gate_num, GROUP_TOK, DOCS)
    all_tokens = N_DP * GROUP_TOK
    all_rows = all_tokens * TOPK
    most_rows = N_DP * N_EXPERT * CAP
    flat_input = hidden_in.reshape(all_tokens, D)
    flat_grad = out_grad.reshape(all_tokens, D)
    flat_routes = routes.reshape(all_rows).astype(jnp.int32)
    flat_factor = factor.reshape(all_rows)
    row_ids = jnp.arange(all_rows, dtype=jnp.int32)
    slot_ids = jnp.arange(most_rows, dtype=jnp.int32)

    def one_expert(total, expert_id):
        chosen = flat_routes == expert_id
        count = jnp.sum(chosen.astype(jnp.int32))
        rank = (jnp.cumsum(chosen.astype(jnp.int32)) - 1).astype(jnp.int32)
        target = jnp.where(chosen, rank, most_rows).astype(jnp.int32)
        picked = jnp.zeros((most_rows,), jnp.int32).at[target].set(row_ids, mode='drop')
        valid = slot_ids < count
        token_index = (picked // TOPK).astype(jnp.int32)
        dispatched_rows = jnp.where(valid[:, None], flat_input[token_index], jnp.zeros((), jnp.bfloat16))
        scale_rows = jnp.where(valid, flat_factor[picked], jnp.float32(0.0))
        gradient_row_block = (scale_rows[:, None] * flat_grad[token_index].astype(jnp.float32)).astype(jnp.bfloat16)
        per_row_gradient, gradient_tuple = expert_rows(dispatched_rows, gradient_row_block, w_gate[expert_id], w_up[expert_id], w_down[expert_id], a_gate[expert_id], b_gate[expert_id], a_up[expert_id], b_up[expert_id], a_down[expert_id], b_down[expert_id])
        added = jnp.where(valid[:, None], per_row_gradient.astype(jnp.float32), jnp.float32(0.0))
        total = total.at[token_index].add(added)
        return (total, gradient_tuple)
    start = jnp.zeros((all_tokens, D), jnp.float32)
    total, gradient_tuple = lax.scan(one_expert, start, jnp.arange(EXPERTS, dtype=jnp.int32))
    input_grad = total.reshape(N_DP, GROUP_TOK, D).astype(jnp.bfloat16)
    return (input_grad, gradient_tuple[0], gradient_tuple[1], gradient_tuple[2], gradient_tuple[3], gradient_tuple[4], gradient_tuple[5])
```

```python
import jax
import jax.numpy as jnp
from jax import lax
from jax.experimental import pallas as pl
from jax.experimental.pallas import tpu as pltpu
from jax.sharding import PartitionSpec as P


SCALE = 2.0
F32 = jnp.float32
BF16 = jnp.bfloat16
LANES = 128

NN = (((1,), (0,)), ((), ()))
NT = (((1,), (1,)), ((), ()))
TN = (((0,), (0,)), ((), ()))


def dot(left, right, dims=NN):
    return lax.dot_general(left, right, dims, preferred_element_type=F32)


def vmem():
    return pl.BlockSpec(memory_space=pltpu.VMEM)


def smem():
    return pl.BlockSpec(memory_space=pltpu.SMEM)


def anyspace():
    return pl.BlockSpec(memory_space=pl.ANY)


def call(body, ins, in_specs, outs, out_specs, scratch, flops, nbytes, name):
    return pl.pallas_call(
        body,
        out_shape=[jax.ShapeDtypeStruct(s, d) for s, d in outs],
        in_specs=in_specs,
        out_specs=out_specs,
        scratch_shapes=scratch,
        compiler_params=pltpu.CompilerParams(vmem_limit_bytes=60 * 1024 * 1024),
        cost_estimate=pl.CostEstimate(flops=flops, bytes_accessed=nbytes, transcendentals=0),
        name=name,
    )(*ins)


def choice_masks(routes_ref, experts, tokens):
    expert_id = lax.broadcasted_iota(jnp.int32, (experts, tokens), 0)
    first = routes_ref[0:1, :] == expert_id
    second = routes_ref[1:2, :] == expert_id
    either = first | second
    earlier = lax.broadcasted_iota(jnp.int32, (tokens, tokens), 0) < lax.broadcasted_iota(
        jnp.int32, (tokens, tokens), 1
    )
    rank = dot(jnp.where(either, 1.0, 0.0).astype(BF16), jnp.where(earlier, 1.0, 0.0).astype(BF16))
    return first, second, either, rank


def dispatch_body(slots, group_tokens, doc_count):
    def body(routes_ref, nums_ref, lengths_ref, start_ref, x_ref, g_ref, send_ref, wide):
        experts = send_ref.shape[0]
        tokens, features = x_ref.shape
        tiles = features // LANES
        depth = 2 * slots * tiles
        first, second, either, rank = choice_masks(routes_ref, experts, tokens)
        position = start_ref[0] + lax.broadcasted_iota(jnp.int32, (1, tokens), 1)
        own = jnp.zeros((1, tokens), jnp.int32)
        begin = jnp.int32(0)
        for j in range(doc_count):
            length = lengths_ref[0, j]
            own = jnp.where((position >= begin) & (position < begin + length), length, own)
            begin = begin + length
        weight = jnp.sqrt(jnp.float32(group_tokens) / (doc_count * own).astype(F32))
        factor = nums_ref[...].astype(F32) / 1024.0 * weight
        factors = jnp.where(first, factor[0:1, :], 0.0) + jnp.where(second, factor[1:2, :], 0.0)
        for c in range(slots):
            chosen = jnp.where(either & (rank == float(c)), 1.0, 0.0)
            scale = jnp.sum(chosen * factors, axis=1, keepdims=True)
            pick = chosen.astype(BF16)
            for j in range(tiles):
                cols = slice(j * LANES, (j + 1) * LANES)
                wide[pl.ds(c * tiles + j, experts, stride=depth), :] = dot(pick, x_ref[:, cols])
                wide[pl.ds((slots + c) * tiles + j, experts, stride=depth), :] = scale * dot(
                    pick, g_ref[:, cols]
                )

        @pl.loop(0, experts // 8)
        def _(i):
            rows = pl.multiple_of(i * 8 * depth, 8 * depth)
            send_ref[pl.ds(i * 8, 8)] = (
                wide[pl.ds(rows, 8 * depth), :].astype(BF16).reshape(8, depth, LANES)
            )

    return body


def expert_body(slots, share):
    half = share // 2

    def body(
        recv_ref,
        *refs,
    ):
        weight_refs = refs[:15]
        left_ref, bdown_ref, right_ref = refs[15:18]
        send_ref, rows_out, acts_out, lows_ref = refs[18:22]
        wide, rows, acts, weights, sems, osems = refs[22:]
        peers = recv_ref.shape[0]
        features = rows.shape[2]
        hidden = acts.shape[2]
        tiles = features // LANES
        depth = 2 * slots * tiles
        count = slots * peers
        copies = []
        for m in range(3):
            own, ahead, far_a, far_b, behind = weight_refs[5 * m : 5 * m + 5]
            parts = (
                (own, 0, share),
                (ahead, share, share),
                (far_a, 2 * share, half),
                (far_b, 2 * share + half, half),
                (behind, 3 * share, share),
            )
            for k, (ref, at, size) in enumerate(parts):
                copies.append(
                    pltpu.make_async_copy(ref, weights.at[m, pl.ds(at, size)], sems.at[m, k])
                )
        for copy in copies:
            copy.start()

        @pl.loop(0, peers // 8)
        def _(i):
            at = pl.multiple_of(i * 8 * depth, 8 * depth)
            wide[pl.ds(at, 8 * depth), :] = (
                recv_ref[pl.ds(i * 8, 8)].astype(F32).reshape(8 * depth, LANES)
            )

        for side in range(2):
            for c in range(slots):
                for j in range(tiles):
                    rows[side, c * peers : (c + 1) * peers, j * LANES : (j + 1) * LANES] = wide[
                        pl.ds((side * slots + c) * tiles + j, peers, stride=depth), :
                    ].astype(BF16)
        out_copies = [pltpu.make_async_copy(rows, rows_out, osems.at[0])]
        out_copies[0].start()
        x = rows.at[0]
        s = rows.at[1]
        lows = dot(x[...], left_ref[...], NT)
        gate_low = lows[:, :16].astype(BF16)
        up_low = lows[:, 16:].astype(BF16)
        grad_low = dot(s[...], bdown_ref[...], NT).astype(BF16)
        for copy in copies:
            copy.wait()
        chunk = 256
        for n in range(hidden // chunk):
            cols = slice(n * chunk, (n + 1) * chunk)
            gate = dot(x[...], weights[0, cols, :], NT) + SCALE * dot(gate_low, right_ref[0, :, cols])
            up = dot(x[...], weights[1, cols, :], NT) + SCALE * dot(up_low, right_ref[1, :, cols])
            back = dot(s[...], weights[2, cols, :], NT) + SCALE * dot(grad_low, right_ref[2, :, cols])
            sigma = jax.nn.sigmoid(gate)
            active = gate * sigma
            acts[0, :, cols] = (active * up).astype(BF16)
            acts[1, :, cols] = (back * up * sigma * (1.0 + gate * (1.0 - sigma))).astype(BF16)
            acts[2, :, cols] = (back * active).astype(BF16)
        out_copies.append(pltpu.make_async_copy(acts, acts_out, osems.at[1]))
        out_copies[1].start()
        gate_back = dot(acts[1], right_ref[0], NT).astype(BF16)
        up_back = dot(acts[2], right_ref[1], NT).astype(BF16)
        for j in range(features // chunk):
            cols = slice(j * chunk, (j + 1) * chunk)
            part = (
                dot(acts[1], weights[0, :, cols])
                + dot(acts[2], weights[1, :, cols])
                + SCALE * (dot(gate_back, left_ref[0:16, cols]) + dot(up_back, left_ref[16:32, cols]))
            )
            for c in range(slots):
                for h in range(chunk // LANES):
                    wide[
                        pl.ds(c * tiles + j * (chunk // LANES) + h, peers, stride=slots * tiles), :
                    ] = part[c * peers : (c + 1) * peers, h * LANES : (h + 1) * LANES]

        @pl.loop(0, peers // 8)
        def _(i):
            step = 8 * slots * tiles
            at = pl.multiple_of(i * step, step)
            send_ref[pl.ds(i * 8, 8)] = (
                wide[pl.ds(at, step), :].astype(BF16).reshape(8, slots * tiles, LANES)
            )

        for k, low in enumerate((gate_low, up_low, grad_low, gate_back, up_back)):
            lows_ref[k] = low
        for copy in out_copies:
            copy.wait()

    return body


def adapter_body(slots, share, width):
    def body(me_ref, routes_ref, rows_ref, acts_ref, lows_ref, right_ref, *refs):
        shares = refs[:4]
        back_ref = refs[4]
        big, small = refs[5:]
        tokens = routes_ref.shape[1]
        experts = tokens
        down_low = dot(acts_ref[0], right_ref[2], NT).astype(BF16)
        big[0] = SCALE * dot(lows_ref[3], rows_ref[0], TN)
        big[1] = SCALE * dot(lows_ref[4], rows_ref[0], TN)
        big[2] = SCALE * dot(down_low, rows_ref[1], TN)
        small[0] = SCALE * dot(lows_ref[0], acts_ref[1], TN)
        small[1] = SCALE * dot(lows_ref[1], acts_ref[2], TN)
        small[2] = SCALE * dot(lows_ref[2], acts_ref[0], TN)
        for k in range(4):
            at = pl.multiple_of(((me_ref[0] + k) % 4) * width, width)
            for m in range(3):
                shares[k][m, :, 0:width] = big[m, :, pl.ds(at, width)]
                shares[k][m, :, width : width + share] = small[m, :, k * share : (k + 1) * share]
                shares[k][m, :, width + share :] = jnp.zeros((16, 256 - share), F32)
        _, _, either, rank = choice_masks(routes_ref, experts, tokens)
        for c in range(slots):
            back_ref[:, c * experts : (c + 1) * experts] = jnp.where(
                either & (rank == float(c)), 1.0, 0.0
            ).T.astype(BF16)

    return body


def total_body(share, width):
    def body(a_ref, b_ref, c_ref, d_ref, *outs):
        for m in range(3):
            total = a_ref[m] + b_ref[m] + c_ref[m] + d_ref[m]
            outs[m][...] = total[:, :width]
            outs[3 + m][...] = total[:, width : width + share]

    return body


def combine_body(slots):
    def body(back_ref, pick_ref, out_ref, wide, rows):
        experts = back_ref.shape[0]
        tokens, features = out_ref.shape
        tiles = features // LANES
        depth = slots * tiles

        @pl.loop(0, experts // 8)
        def _(i):
            at = pl.multiple_of(i * 8 * depth, 8 * depth)
            wide[pl.ds(at, 8 * depth), :] = (
                back_ref[pl.ds(i * 8, 8)].astype(F32).reshape(8 * depth, LANES)
            )

        for j in range(tiles):
            for c in range(slots):
                rows[c * experts : (c + 1) * experts, j * LANES : (j + 1) * LANES] = wide[
                    pl.ds(c * tiles + j, experts, stride=depth), :
                ].astype(BF16)
        for j in range(0, features, 256):
            out_ref[:, j : j + 256] = dot(pick_ref[...], rows[:, j : j + 256]).astype(BF16)

    return body


def on_device(
    hidden_in,
    out_grad,
    routes,
    gate_num,
    doc_lengths,
    w_gate,
    w_up,
    w_down,
    a_gate,
    b_gate,
    a_up,
    b_up,
    a_down,
    b_down,
):
    tokens, features = hidden_in.shape[1:]
    groups = lax.axis_size("expert")
    shards = lax.axis_size("dp")
    share = w_gate.shape[1]
    hidden = share * shards
    rank_dim = a_gate.shape[2]
    width = features // shards
    slots = min(tokens, max(2, 3 * tokens * routes.shape[2] // (2 * groups)))
    tiles = features // LANES
    depth = slots * tiles
    rows = slots * groups
    me = lax.axis_index("dp")
    routes_t = routes[0].T
    start = (lax.axis_index("expert") * tokens).astype(jnp.int32).reshape(1)
    x, g = hidden_in[0], out_grad[0]

    (send,) = call(
        dispatch_body(slots, tokens * groups, doc_lengths.shape[1]),
        (routes_t, gate_num[0].T, doc_lengths, start, x, g),
        [vmem(), vmem(), smem(), smem(), vmem(), vmem()],
        [((groups, 2 * depth, LANES), BF16)],
        [vmem()],
        [pltpu.VMEM((groups * 2 * depth, LANES), F32)],
        4 * rows * tokens * features,
        4 * rows * features,
        "dispatch",
    )
    own = (w_gate[0], w_up[0], w_down[0])
    send, own = lax.optimization_barrier((send, own))
    with jax.named_scope("rowsout"):
        recv = lax.all_to_all(send, "expert", split_axis=0, concat_axis=0, tiled=True)

    up_ring = [(i, (i + 1) % shards) for i in range(shards)]
    down_ring = [(i, (i - 1) % shards) for i in range(shards)]
    with jax.named_scope("ring"):
        behind = [lax.ppermute(w, "dp", up_ring) for w in own]
        ahead = [lax.ppermute(w, "dp", down_ring) for w in own]
        far_a = [lax.ppermute(w[: share // 2], "dp", up_ring) for w in behind]
        far_b = [lax.ppermute(w[share // 2 :], "dp", down_ring) for w in ahead]
    weights = []
    for m in range(3):
        weights += [own[m], ahead[m], far_a[m], far_b[m], behind[m]]

    left = jnp.concatenate([a_gate[0].T, a_up[0].T], axis=0)
    right = jnp.stack([b_gate[0], b_up[0], a_down[0].T])
    right = lax.dynamic_slice_in_dim(
        jnp.concatenate([right, right], axis=2), me * share, hidden, axis=2
    )
    send_back, row_blocks, acts, lows = call(
        expert_body(slots, share),
        (recv, *weights, left, b_down[0], right),
        [vmem()] + [anyspace()] * 15 + [vmem()] * 3,
        [
            ((groups, depth, LANES), BF16),
            ((2, rows, features), BF16),
            ((3, rows, hidden), BF16),
            ((5, rows, rank_dim), BF16),
        ],
        [vmem(), anyspace(), anyspace(), vmem()],
        [
            pltpu.VMEM((groups * 2 * depth, LANES), F32),
            pltpu.VMEM((2, rows, features), BF16),
            pltpu.VMEM((3, rows, hidden), BF16),
            pltpu.VMEM((3, hidden, features), BF16),
            pltpu.SemaphoreType.DMA((3, 5)),
            pltpu.SemaphoreType.DMA((2,)),
        ],
        10 * rows * hidden * features,
        6 * hidden * features + 6 * rows * features,
        "experts",
    )
    with jax.named_scope("rowsback"):
        back = lax.all_to_all(send_back, "expert", split_axis=0, concat_axis=0, tiled=True)

    *shares, pick = call(
        adapter_body(slots, share, width),
        (me.astype(jnp.int32).reshape(1), routes_t, row_blocks, acts, lows, right),
        [smem()] + [vmem()] * 5,
        [((3, rank_dim, width + 256), F32)] * 4 + [((tokens, rows), BF16)],
        [vmem()] * 5,
        [pltpu.VMEM((3, rank_dim, features), F32), pltpu.VMEM((3, rank_dim, hidden), F32)],
        12 * rows * features * rank_dim,
        4 * rows * features,
        "adapters",
    )
    with jax.named_scope("adapterring"):
        parts = [shares[0]] + [
            lax.ppermute(shares[k], "dp", [(i, (i + k) % shards) for i in range(shards)])
            for k in range(1, shards)
        ]
    big_gate, big_up, big_down, small_gate, small_up, small_down = call(
        total_body(share, width),
        parts,
        [vmem()] * 4,
        [((rank_dim, width), F32)] * 3 + [((rank_dim, share), F32)] * 3,
        [vmem()] * 6,
        [],
        9 * rank_dim * (width + share),
        60 * rank_dim * (width + share),
        "totals",
    )
    (input_grad,) = call(
        combine_body(slots),
        (back, pick),
        [vmem()] * 2,
        [((tokens, features), BF16)],
        [vmem()],
        [pltpu.VMEM((groups * depth, LANES), F32), pltpu.VMEM((rows, features), BF16)],
        2 * rows * tokens * features,
        2 * rows * features,
        "combine",
    )
    return (
        input_grad[None],
        big_gate.T[None],
        small_gate[None],
        big_up.T[None],
        small_up[None],
        small_down.T[None],
        big_down[None],
    )


def solution(mesh):
    return jax.shard_map(
        on_device,
        mesh=mesh,
        in_specs=(
            P("dp", "expert", None),
            P("dp", "expert", None),
            P("dp", "expert", None),
            P("dp", "expert", None),
            P("dp", None),
            P("expert", "dp", None),
            P("expert", "dp", None),
            P("expert", "dp", None),
            P("expert", None, None),
            P("expert", None, None),
            P("expert", None, None),
            P("expert", None, None),
            P("expert", None, None),
            P("expert", None, None),
        ),
        out_specs=(
            P("dp", "expert", None),
            P("expert", "dp", None),
            P("expert", None, "dp"),
            P("expert", "dp", None),
            P("expert", None, "dp"),
            P("expert", "dp", None),
            P("expert", None, "dp"),
        ),
        check_vma=False,
    )
```

```python
import jax
import jax.numpy as jnp
from jax import lax
from jax.experimental import pallas as pl
from jax.experimental.pallas import tpu as pltpu
from jax.sharding import PartitionSpec as P


SCALE = 2.0
F32 = jnp.float32
BF16 = jnp.bfloat16
LANES = 128

NN = (((1,), (0,)), ((), ()))
NT = (((1,), (1,)), ((), ()))
TN = (((0,), (0,)), ((), ()))


def dot(left, right, dims=NN):
    return lax.dot_general(left, right, dims, preferred_element_type=F32)


def vmem():
    return pl.BlockSpec(memory_space=pltpu.VMEM)


def in_hbm(arrays):
    return [pltpu.with_memory_space_constraint(a, pltpu.HBM) for a in arrays]


def smem():
    return pl.BlockSpec(memory_space=pltpu.SMEM)


def anyspace():
    return pl.BlockSpec(memory_space=pl.ANY)


def call(body, ins, in_specs, outs, out_specs, scratch, flops, nbytes, mib):
    return pl.pallas_call(
        body,
        out_shape=[space(s, d) for s, d, space in outs],
        in_specs=in_specs,
        out_specs=out_specs,
        scratch_shapes=scratch,
        compiler_params=pltpu.CompilerParams(vmem_limit_bytes=mib * 1024 * 1024),
        cost_estimate=pl.CostEstimate(flops=flops, bytes_accessed=nbytes, transcendentals=0),
    )(*ins)


def pack_blocks(wide, stage, out_ref, sems, pitch):
    blocks, depth, _ = stage.shape

    def copy_of(i):
        some = pl.ds(i * 8, 8)
        return pltpu.make_async_copy(stage.at[some], out_ref.at[some], sems.at[i])

    @pl.loop(0, blocks // 8)
    def _(i):
        for e in range(8):
            at = pl.multiple_of(i * 8 * pitch, 8) + e * pitch
            stage[i * 8 + e] = wide[pl.ds(at, depth), :].astype(BF16)
        copy_of(i).start()

    @pl.loop(0, blocks // 8)
    def _(i):
        copy_of(i).wait()


def unpack_blocks(in_ref, wide, pitch):
    blocks, depth, _ = in_ref.shape

    @pl.loop(0, blocks // 8)
    def _(i):
        for e in range(8):
            at = pl.multiple_of(i * 8 * pitch, 8) + e * pitch
            wide[pl.ds(at, depth), :] = in_ref[i * 8 + e].astype(F32)


def choice_masks(routes_ref, experts, tokens):
    expert_id = lax.broadcasted_iota(jnp.int32, (experts, tokens), 0)
    first = routes_ref[0:1, :] == expert_id
    second = routes_ref[1:2, :] == expert_id
    either = first | second
    earlier = lax.broadcasted_iota(jnp.int32, (tokens, tokens), 0) < lax.broadcasted_iota(
        jnp.int32, (tokens, tokens), 1
    )
    rank = dot(jnp.where(either, 1.0, 0.0).astype(BF16), jnp.where(earlier, 1.0, 0.0).astype(BF16))
    return first, second, either, rank


def dispatch_body(slots, group_tokens, doc_count):
    def body(routes_ref, nums_ref, lengths_ref, start_ref, x_hbm, g_hbm, send_ref, wide, stage, x_ref, g_ref, lsems, sems):
        loads = [
            pltpu.make_async_copy(x_hbm, x_ref, lsems.at[0]),
            pltpu.make_async_copy(g_hbm, g_ref, lsems.at[1]),
        ]
        for load in loads:
            load.start()
        experts = stage.shape[0]
        tokens, features = x_ref.shape
        tiles = features // LANES
        depth = 2 * slots * tiles
        pitch = depth + 4
        first, second, either, rank = choice_masks(routes_ref, experts, tokens)
        position = start_ref[0] + lax.broadcasted_iota(jnp.int32, (1, tokens), 1)
        own = jnp.zeros((1, tokens), jnp.int32)
        begin = jnp.int32(0)
        for j in range(doc_count):
            length = lengths_ref[0, j]
            own = jnp.where((position >= begin) & (position < begin + length), length, own)
            begin = begin + length
        weight = jnp.sqrt(jnp.float32(group_tokens) / (doc_count * own).astype(F32))
        factor = nums_ref[...].astype(F32) / 1024.0 * weight
        factors = jnp.where(first, factor[0:1, :], 0.0) + jnp.where(second, factor[1:2, :], 0.0)
        picks, scales = [], []
        for c in range(slots):
            chosen = jnp.where(either & (rank == float(c)), 1.0, 0.0)
            scales.append(jnp.sum(chosen * factors, axis=1, keepdims=True))
            picks.append(chosen.astype(BF16))
        pick = jnp.concatenate(picks, axis=0)
        scale = jnp.concatenate(scales, axis=0)
        for load in loads:
            load.wait()
        chunk = 2 * LANES
        for j in range(features // chunk):
            cols = slice(j * chunk, (j + 1) * chunk)
            both = (dot(pick, x_ref[:, cols]), scale * dot(pick, g_ref[:, cols]))
            for side in range(2):
                for c in range(slots):
                    for h in range(2):
                        wide[pl.ds((side * slots + c) * tiles + 2 * j + h, experts, stride=pitch), :] = both[
                            side
                        ][c * experts : (c + 1) * experts, h * LANES : (h + 1) * LANES]
        pack_blocks(wide, stage, send_ref, sems, pitch)

    return body


def expert_body(slots, places):
    def body(recv_ref, *refs):
        weight_refs, refs = refs[: len(places)], refs[len(places) :]
        left_ref, bdown_ref, right_ref, send_ref, rows_out, acts_out, lows_ref = refs[:7]
        wide, more, x, s, gates, ups, acts, weights, backs, stage, sems, osems, ssems = refs[7:]
        peers = recv_ref.shape[0]
        features = x.shape[1]
        hidden = acts.shape[2]
        tiles = features // LANES
        depth = slots * tiles
        pitch = depth + 4
        narrow = tiles + 4
        copies = [[], [], []]
        for k, (ref, (m, at, size)) in enumerate(zip(weight_refs, places)):
            copies[m].append(
                pltpu.make_async_copy(ref, weights.at[m, pl.ds(at, size)], sems.at[k])
            )
        for m in range(3):
            for copy in copies[m]:
                copy.start()

        for e in range(peers):
            wide[e * pitch : e * pitch + depth, :] = recv_ref[e, :depth, :].astype(F32)
        for j in range(tiles):
            for c in range(slots):
                x[c * peers : (c + 1) * peers, j * LANES : (j + 1) * LANES] = wide[
                    pl.ds(c * tiles + j, peers, stride=pitch), :
                ].astype(BF16)

        chunk = 256
        chunks = [slice(n * chunk, (n + 1) * chunk) for n in range(hidden // chunk)]
        for copy in copies[0]:
            copy.wait()
        lows = dot(x[...], left_ref[...], NT)
        gate_low = lows[:, :16].astype(BF16)
        up_low = lows[:, 16:].astype(BF16)
        lows_ref[0] = gate_low
        lows_ref[1] = up_low

        @pl.loop(0, slots)
        def _(c):
            cols = pl.ds(pl.multiple_of(c * chunk, chunk), chunk)
            gates[:, cols] = dot(x[...], weights[0, cols, :], NT) + SCALE * dot(
                lows_ref[0], right_ref[0, :, cols]
            )
            from_row = pl.multiple_of(depth + c * tiles, tiles)
            for e in range(peers):
                more[e * narrow : e * narrow + tiles, :] = recv_ref[e, pl.ds(from_row, tiles), :].astype(F32)
            for j in range(tiles):
                s[pl.ds(pl.multiple_of(c * peers, peers), peers), j * LANES : (j + 1) * LANES] = more[
                    pl.ds(j, peers, stride=narrow), :
                ].astype(BF16)

        for copy in copies[1]:
            copy.wait()
        out_copies = [
            pltpu.make_async_copy(x, rows_out.at[0], osems.at[0]),
            pltpu.make_async_copy(s, rows_out.at[1], osems.at[1]),
        ]
        for copy in out_copies:
            copy.start()
        for cols in chunks:
            ups[:, cols] = dot(x[...], weights[1, cols, :], NT) + SCALE * dot(
                lows_ref[1], right_ref[1, :, cols]
            )
        grad_low = dot(s[...], bdown_ref[...], NT).astype(BF16)
        lows_ref[2] = grad_low
        for copy in copies[2]:
            copy.wait()
        for cols in chunks:
            gate, up = gates[:, cols], ups[:, cols]
            back = dot(s[...], weights[2, cols, :], NT) + SCALE * dot(
                lows_ref[2], right_ref[2, :, cols]
            )
            sigma = jax.nn.sigmoid(gate)
            active = gate * sigma
            acts[0, :, cols] = (active * up).astype(BF16)
            acts[1, :, cols] = (back * up * sigma * (1.0 + gate * (1.0 - sigma))).astype(BF16)
            acts[2, :, cols] = (back * active).astype(BF16)
        out_copies.append(pltpu.make_async_copy(acts, acts_out, osems.at[2]))
        out_copies[2].start()
        gate_back = dot(acts[1], right_ref[0], NT).astype(BF16)
        up_back = dot(acts[2], right_ref[1], NT).astype(BF16)
        backs[:, :16] = gate_back
        backs[:, 16:] = up_back
        for j in range(features // chunk):
            cols = slice(j * chunk, (j + 1) * chunk)
            part = (
                dot(acts[1], weights[0, :, cols])
                + dot(acts[2], weights[1, :, cols])
                + SCALE * dot(backs[...], left_ref[:, cols])
            )
            for c in range(slots):
                for h in range(chunk // LANES):
                    wide[
                        pl.ds(c * tiles + j * (chunk // LANES) + h, peers, stride=pitch), :
                    ] = part[c * peers : (c + 1) * peers, h * LANES : (h + 1) * LANES]

        lows_ref[3] = gate_back
        lows_ref[4] = up_back
        pack_blocks(wide, stage, send_ref, ssems, pitch)
        for copy in out_copies:
            copy.wait()

    return body


def adapter_body(slots, share, width):
    def body(me_ref, routes_ref, rows_ref, acts_ref, lows_ref, right_ref, *refs):
        shares = refs[:4]
        back_ref = refs[4]
        big, small = refs[5:]
        tokens = routes_ref.shape[1]
        experts = tokens
        down_low = dot(acts_ref[0], right_ref[2], NT).astype(BF16)
        big[0] = SCALE * dot(lows_ref[3], rows_ref[0], TN)
        big[1] = SCALE * dot(lows_ref[4], rows_ref[0], TN)
        big[2] = SCALE * dot(down_low, rows_ref[1], TN)
        small[0] = SCALE * dot(lows_ref[0], acts_ref[1], TN)
        small[1] = SCALE * dot(lows_ref[1], acts_ref[2], TN)
        small[2] = SCALE * dot(lows_ref[2], acts_ref[0], TN)
        for k in range(4):
            at = pl.multiple_of(((me_ref[0] + k) % 4) * width, width)
            for m in range(3):
                shares[k][m, :, 0:width] = big[m, :, pl.ds(at, width)]
                shares[k][m, :, width : width + share] = small[m, :, k * share : (k + 1) * share]
                shares[k][m, :, width + share :] = jnp.zeros((16, 256 - share), F32)
        _, _, either, rank = choice_masks(routes_ref, experts, tokens)
        for c in range(slots):
            back_ref[:, c * experts : (c + 1) * experts] = jnp.where(
                either & (rank == float(c)), 1.0, 0.0
            ).T.astype(BF16)

    return body


def total_body(share, width):
    def body(a_ref, b_ref, c_ref, d_ref, *outs):
        for m in range(3):
            total = a_ref[m] + b_ref[m] + c_ref[m] + d_ref[m]
            outs[m][...] = total[:, :width]
            outs[3 + m][...] = total[:, width : width + share]

    return body


def combine_body(slots):
    def body(back_ref, pick_ref, out_ref, wide, rows):
        experts = back_ref.shape[0]
        _, features = out_ref.shape
        tiles = features // LANES
        depth = slots * tiles

        unpack_blocks(back_ref, wide, depth + 4)
        for j in range(tiles):
            for c in range(slots):
                rows[c * experts : (c + 1) * experts, j * LANES : (j + 1) * LANES] = wide[
                    pl.ds(c * tiles + j, experts, stride=depth + 4), :
                ].astype(BF16)
        for j in range(0, features, 256):
            out_ref[:, j : j + 256] = dot(pick_ref[...], rows[:, j : j + 256]).astype(BF16)

    return body


def layer(
    hidden_in,
    out_grad,
    routes,
    gate_num,
    doc_lengths,
    w_gate,
    w_up,
    w_down,
    a_gate,
    b_gate,
    a_up,
    b_up,
    a_down,
    b_down,
):
    tokens, features = hidden_in.shape[1:]
    groups = lax.axis_size("expert")
    shards = lax.axis_size("dp")
    share = w_gate.shape[1]
    hidden = share * shards
    rank_dim = a_gate.shape[2]
    width = features // shards
    slots = min(tokens, max(2, 3 * tokens * routes.shape[2] // (2 * groups)))
    tiles = features // LANES
    depth = slots * tiles
    rows = slots * groups
    me = lax.axis_index("dp")
    routes_t = routes[0].T
    start = (lax.axis_index("expert") * tokens).astype(jnp.int32).reshape(1)
    x, g = hidden_in[0], out_grad[0]

    up_ring = [(i, (i + 1) % shards) for i in range(shards)]
    down_ring = [(i, (i - 1) % shards) for i in range(shards)]
    early = lax.ppermute(w_gate[0], "dp", up_ring)
    (send,) = call(
        dispatch_body(slots, tokens * groups, doc_lengths.shape[1]),
        (*in_hbm((routes_t, gate_num[0].T, doc_lengths)), start, *in_hbm((x, g))),
        [vmem(), vmem(), smem(), smem(), anyspace(), anyspace()],
        [((groups, 2 * depth, LANES), BF16, pltpu.HBM)],
        [anyspace()],
        [
            pltpu.VMEM((groups * (2 * depth + 4), LANES), F32),
            pltpu.VMEM((groups, 2 * depth, LANES), BF16),
            pltpu.VMEM((tokens, features), BF16),
            pltpu.VMEM((tokens, features), BF16),
            pltpu.SemaphoreType.DMA((2,)),
            pltpu.SemaphoreType.DMA((groups // 8,)),
        ],
        4 * rows * tokens * features,
        4 * rows * features,
        16,
    )
    send, gate_late, w_up_late, w_down_late = lax.optimization_barrier(
        (send, w_gate[0], w_up[0], w_down[0])
    )
    own = (w_gate[0], w_up[0], w_down[0])
    late = (gate_late, w_up_late, w_down_late)
    recv = lax.all_to_all(send, "expert", split_axis=0, concat_axis=0, tiled=True)

    half = share // 2
    behind = [early] + [lax.ppermute(w, "dp", up_ring) for w in late[1:]]
    ahead = [lax.ppermute(w, "dp", down_ring) for w in late]
    far = [[lax.ppermute(behind[0], "dp", up_ring)]] + [
        [lax.ppermute(behind[m][:half], "dp", up_ring), lax.ppermute(ahead[m][half:], "dp", down_ring)]
        for m in (1, 2)
    ]
    weights, places = [], []
    for m in range(3):
        weights += [own[m], ahead[m], behind[m], *far[m]]
        places += [(m, 0, share), (m, share, share), (m, 3 * share, share)]
        size = share // len(far[m])
        places += [(m, 2 * share + k * size, size) for k in range(len(far[m]))]

    left = jnp.concatenate([a_gate[0].T, a_up[0].T], axis=0)
    right = jnp.stack([b_gate[0], b_up[0], a_down[0].T])
    right = lax.dynamic_slice_in_dim(
        jnp.concatenate([right, right], axis=2), me * share, hidden, axis=2
    )
    send_back, row_blocks, acts, lows = call(
        expert_body(slots, places),
        (recv, *in_hbm((*weights, left, b_down[0], right))),
        [vmem()] + [anyspace()] * len(weights) + [vmem()] * 3,
        [
            ((groups, depth, LANES), BF16, pltpu.HBM),
            ((2, rows, features), BF16, pltpu.HBM),
            ((3, rows, hidden), BF16, pltpu.HBM),
            ((5, rows, rank_dim), BF16, pltpu.HBM),
        ],
        [anyspace(), anyspace(), anyspace(), vmem()],
        [
            pltpu.VMEM((groups * (depth + 4), LANES), F32),
            pltpu.VMEM((groups * (tiles + 4), LANES), F32),
            pltpu.VMEM((rows, features), BF16),
            pltpu.VMEM((rows, features), BF16),
            pltpu.VMEM((rows, hidden), F32),
            pltpu.VMEM((rows, hidden), F32),
            pltpu.VMEM((3, rows, hidden), BF16),
            pltpu.VMEM((3, hidden, features), BF16),
            pltpu.VMEM((rows, 2 * rank_dim), BF16),
            pltpu.VMEM((groups, depth, LANES), BF16),
            pltpu.SemaphoreType.DMA((len(places),)),
            pltpu.SemaphoreType.DMA((3,)),
            pltpu.SemaphoreType.DMA((groups // 8,)),
        ],
        10 * rows * hidden * features,
        6 * hidden * features + 6 * rows * features,
        40,
    )
    back = lax.all_to_all(send_back, "expert", split_axis=0, concat_axis=0, tiled=True)

    *shares, pick = call(
        adapter_body(slots, share, width),
        (me.astype(jnp.int32).reshape(1), *in_hbm((routes_t, row_blocks, acts, lows, right))),
        [smem()] + [vmem()] * 5,
        [((3, rank_dim, width + 256), F32, pltpu.HBM)] * 4 + [((tokens, rows), BF16, pltpu.VMEM)],
        [vmem()] * 5,
        [pltpu.VMEM((3, rank_dim, features), F32), pltpu.VMEM((3, rank_dim, hidden), F32)],
        12 * rows * features * rank_dim,
        4 * rows * features,
        12,
    )
    parts = [shares[0]] + [
        lax.ppermute(shares[k], "dp", [(i, (i + k) % shards) for i in range(shards)])
        for k in range(1, shards)
    ]
    big_gate, big_up, big_down, small_gate, small_up, small_down = call(
        total_body(share, width),
        parts,
        [vmem()] * 4,
        [((rank_dim, width), F32, pltpu.HBM)] * 3 + [((rank_dim, share), F32, pltpu.HBM)] * 3,
        [vmem()] * 6,
        [],
        9 * rank_dim * (width + share),
        60 * rank_dim * (width + share),
        4,
    )
    (input_grad,) = call(
        combine_body(slots),
        (back, pltpu.with_memory_space_constraint(pick, pltpu.VMEM)),
        [vmem()] * 2,
        [((tokens, features), BF16, pltpu.HBM)],
        [vmem()],
        [pltpu.VMEM((groups * (depth + 4), LANES), F32), pltpu.VMEM((rows, features), BF16)],
        2 * rows * tokens * features,
        2 * rows * features,
        12,
    )
    return (
        input_grad[None],
        big_gate.T[None],
        small_gate[None],
        big_up.T[None],
        small_up[None],
        small_down.T[None],
        big_down[None],
    )


def solution(mesh):
    return jax.shard_map(
        layer,
        mesh=mesh,
        in_specs=(
            P("dp", "expert", None),
            P("dp", "expert", None),
            P("dp", "expert", None),
            P("dp", "expert", None),
            P("dp", None),
            P("expert", "dp", None),
            P("expert", "dp", None),
            P("expert", "dp", None),
            P("expert", None, None),
            P("expert", None, None),
            P("expert", None, None),
            P("expert", None, None),
            P("expert", None, None),
            P("expert", None, None),
        ),
        out_specs=(
            P("dp", "expert", None),
            P("expert", "dp", None),
            P("expert", None, "dp"),
            P("expert", "dp", None),
            P("expert", None, "dp"),
            P("expert", "dp", None),
            P("expert", None, "dp"),
        ),
        check_vma=False,
    )
```

```python
import jax
import jax.numpy as jnp
from jax import lax
from jax.experimental import pallas as pl
from jax.experimental.pallas import tpu as pltpu
from jax.sharding import PartitionSpec as P


SCALE = 2.0
F32 = jnp.float32
BF16 = jnp.bfloat16
LANES = 128

NN = (((1,), (0,)), ((), ()))
NT = (((1,), (1,)), ((), ()))
TN = (((0,), (0,)), ((), ()))


def dot(left, right, dims=NN):
    return lax.dot_general(left, right, dims, preferred_element_type=F32)


def vmem():
    return pl.BlockSpec(memory_space=pltpu.VMEM)


def in_hbm(arrays):
    return [pltpu.with_memory_space_constraint(a, pltpu.HBM) for a in arrays]


def in_vmem(arrays):
    return [pltpu.with_memory_space_constraint(a, pltpu.VMEM) for a in arrays]


def smem():
    return pl.BlockSpec(memory_space=pltpu.SMEM)


def anyspace():
    return pl.BlockSpec(memory_space=pl.ANY)


def call(body, ins, in_specs, outs, out_specs, scratch, flops, nbytes, mib):
    return pl.pallas_call(
        body,
        out_shape=[space(s, d) for s, d, space in outs],
        in_specs=in_specs,
        out_specs=out_specs,
        scratch_shapes=scratch,
        compiler_params=pltpu.CompilerParams(vmem_limit_bytes=mib * 1024 * 1024),
        cost_estimate=pl.CostEstimate(flops=flops, bytes_accessed=nbytes, transcendentals=0),
    )(*ins)


def pack_blocks(wide, stage, out_ref, sems, pitch):
    blocks, depth, _ = stage.shape

    def copy_of(i):
        some = pl.ds(i * 8, 8)
        return pltpu.make_async_copy(stage.at[some], out_ref.at[some], sems.at[i])

    @pl.loop(0, blocks // 8)
    def _(i):
        for e in range(8):
            at = pl.multiple_of(i * 8 * pitch, 8) + e * pitch
            stage[i * 8 + e] = wide[pl.ds(at, depth), :].astype(BF16)
        copy_of(i).start()

    @pl.loop(0, blocks // 8)
    def _(i):
        copy_of(i).wait()


def unpack_blocks(in_ref, wide, pitch):
    blocks, depth, _ = in_ref.shape

    @pl.loop(0, blocks // 8)
    def _(i):
        for e in range(8):
            at = pl.multiple_of(i * 8 * pitch, 8) + e * pitch
            wide[pl.ds(at, depth), :] = in_ref[i * 8 + e].astype(F32)


def choice_masks(routes_ref, experts, tokens):
    expert_id = lax.broadcasted_iota(jnp.int32, (experts, tokens), 0)
    first = routes_ref[0:1, :] == expert_id
    second = routes_ref[1:2, :] == expert_id
    either = first | second
    earlier = lax.broadcasted_iota(jnp.int32, (tokens, tokens), 0) < lax.broadcasted_iota(
        jnp.int32, (tokens, tokens), 1
    )
    rank = dot(jnp.where(either, 1.0, 0.0).astype(BF16), jnp.where(earlier, 1.0, 0.0).astype(BF16))
    return first, second, either, rank


def dispatch_body(slots, group_tokens, doc_count):
    def body(routes_ref, nums_ref, lengths_ref, start_ref, x_hbm, g_hbm, send_ref, wide, more, stage, x_ref, g_ref, lsems, sems):
        loads = [
            pltpu.make_async_copy(x_hbm, x_ref, lsems.at[0]),
            pltpu.make_async_copy(g_hbm, g_ref, lsems.at[1]),
        ]
        for load in loads:
            load.start()
        experts = stage.shape[0]
        tokens, features = x_ref.shape
        tiles = features // LANES
        depth = slots * tiles
        pitch = depth + 4
        first, second, either, rank = choice_masks(routes_ref, experts, tokens)
        position = start_ref[0] + lax.broadcasted_iota(jnp.int32, (1, tokens), 1)
        own = jnp.zeros((1, tokens), jnp.int32)
        begin = jnp.int32(0)
        for j in range(doc_count):
            length = lengths_ref[0, j]
            own = jnp.where((position >= begin) & (position < begin + length), length, own)
            begin = begin + length
        weight = jnp.sqrt(jnp.float32(group_tokens) / (doc_count * own).astype(F32))
        factor = nums_ref[...].astype(F32) / 1024.0 * weight
        factors = jnp.where(first, factor[0:1, :], 0.0) + jnp.where(second, factor[1:2, :], 0.0)
        picks, scales = [], []
        for c in range(slots):
            chosen = jnp.where(either & (rank == float(c)), 1.0, 0.0)
            scales.append(jnp.sum(chosen * factors, axis=1, keepdims=True))
            picks.append(chosen.astype(BF16))
        pick = jnp.concatenate(picks, axis=0)
        scale = jnp.concatenate(scales, axis=0)
        chunk = 2 * LANES
        copies = []
        for side, (source, scratch) in enumerate(((x_ref, wide), (g_ref, more))):
            loads[side].wait()
            for j in range(features // chunk):
                part = dot(pick, source[:, j * chunk : (j + 1) * chunk])
                if side == 1:
                    part = scale * part
                for c in range(slots):
                    for h in range(2):
                        scratch[pl.ds(c * tiles + 2 * j + h, experts, stride=pitch), :] = part[
                            c * experts : (c + 1) * experts, h * LANES : (h + 1) * LANES
                        ]
            at = pl.ds(side * depth, depth)
            for i in range(experts // 8):
                for e in range(i * 8, i * 8 + 8):
                    stage[e, at, :] = scratch[e * pitch : e * pitch + depth, :].astype(BF16)
                some = pl.ds(i * 8, 8)
                copies.append(
                    pltpu.make_async_copy(
                        stage.at[some, at], send_ref.at[some, at], sems.at[side, i]
                    )
                )
                copies[-1].start()
        for copy in copies:
            copy.wait()

    return body


def product_body(slots, places):
    def body(recv_ref, *refs):
        weight_refs, refs = refs[: len(places)], refs[len(places) :]
        left_ref, bdown_ref, right_ref, rows_out, s, gates, ups, lows_ref, weights = refs[:9]
        x, wide, more, sems, osems = refs[9:]
        peers = recv_ref.shape[0]
        features = x.shape[1]
        hidden = gates.shape[1]
        tiles = features // LANES
        depth = slots * tiles
        pitch = depth + 4
        narrow = tiles + 4
        copies = start_copies(weight_refs, places, weights, sems)
        for e in range(peers):
            wide[e * pitch : e * pitch + depth, :] = recv_ref[e, :depth, :].astype(F32)
        for j in range(tiles):
            for c in range(slots):
                x[c * peers : (c + 1) * peers, j * LANES : (j + 1) * LANES] = wide[
                    pl.ds(c * tiles + j, peers, stride=pitch), :
                ].astype(BF16)
        chunk = hidden // slots
        for copy in copies[0]:
            copy.wait()
        lows = dot(x[...], left_ref[...], NT)
        lows_ref[0] = lows[:, :16].astype(BF16)
        lows_ref[1] = lows[:, 16:].astype(BF16)

        @pl.loop(0, slots)
        def _(c):
            cols = pl.ds(pl.multiple_of(c * chunk, chunk), chunk)
            gates[:, cols] = dot(x[...], weights[0, cols, :], NT) + SCALE * dot(
                lows_ref[0], right_ref[0, :, cols]
            )
            from_row = pl.multiple_of(depth + c * tiles, tiles)
            for e in range(peers):
                more[e * narrow : e * narrow + tiles, :] = recv_ref[e, pl.ds(from_row, tiles), :].astype(F32)
            for j in range(tiles):
                s[pl.ds(pl.multiple_of(c * peers, peers), peers), j * LANES : (j + 1) * LANES] = more[
                    pl.ds(j, peers, stride=narrow), :
                ].astype(BF16)

        for copy in copies[1]:
            copy.wait()
        out_copies = [
            pltpu.make_async_copy(x, rows_out.at[0], osems.at[0]),
            pltpu.make_async_copy(s, rows_out.at[1], osems.at[1]),
        ]
        for copy in out_copies:
            copy.start()
        for n in range(slots):
            cols = slice(n * chunk, (n + 1) * chunk)
            ups[:, cols] = dot(x[...], weights[1, cols, :], NT) + SCALE * dot(
                lows_ref[1], right_ref[1, :, cols]
            )
        lows_ref[2] = dot(s[...], bdown_ref[...], NT).astype(BF16)
        for copy in out_copies:
            copy.wait()

    return body


def start_copies(refs, places, weights, sems):
    copies = [[] for _ in range(weights.shape[0])]
    for k, (ref, (m, at, size)) in enumerate(zip(refs, places)):
        copies[m].append(pltpu.make_async_copy(ref, weights.at[m, pl.ds(at, size)], sems.at[k]))
        copies[m][-1].start()
    return copies


def expert_body(slots, places):
    def body(s, gates, ups, lows_ref, weights, *refs):
        weight_refs, refs = refs[: len(places)], refs[len(places) :]
        left_ref, right_ref, send_ref, acts_out, lows_out = refs[:5]
        wide, down, acts, all_lows, backs, stage, sems, ssems, osems = refs[5:]
        rows, features = s.shape
        hidden = gates.shape[1]
        peers = rows // slots
        tiles = features // LANES
        pitch = slots * tiles + 4
        chunk = 2 * LANES
        for copy in start_copies(weight_refs, places, down, sems)[0]:
            copy.wait()
        for n in range(hidden // chunk):
            cols = slice(n * chunk, (n + 1) * chunk)
            gate, up = gates[:, cols], ups[:, cols]
            back = dot(s[...], down[0, cols, :], NT) + SCALE * dot(lows_ref[2], right_ref[2, :, cols])
            sigma = jax.nn.sigmoid(gate)
            active = gate * sigma
            acts[0, :, cols] = (active * up).astype(BF16)
            acts[1, :, cols] = (back * up * sigma * (1.0 + gate * (1.0 - sigma))).astype(BF16)
            acts[2, :, cols] = (back * active).astype(BF16)
        gate_back = dot(acts[1], right_ref[0], NT).astype(BF16)
        up_back = dot(acts[2], right_ref[1], NT).astype(BF16)
        all_lows[0:3] = lows_ref[...]
        all_lows[3] = gate_back
        all_lows[4] = up_back
        out_copies = [
            pltpu.make_async_copy(acts, acts_out, osems.at[0]),
            pltpu.make_async_copy(all_lows, lows_out, osems.at[1]),
        ]
        for copy in out_copies:
            copy.start()
        backs[:, :16] = gate_back
        backs[:, 16:] = up_back
        for j in range(features // chunk):
            cols = slice(j * chunk, (j + 1) * chunk)
            part = (
                dot(acts[1], weights[0, :, cols])
                + dot(acts[2], weights[1, :, cols])
                + SCALE * dot(backs[...], left_ref[:, cols])
            )
            for c in range(slots):
                for h in range(chunk // LANES):
                    wide[
                        pl.ds(c * tiles + j * (chunk // LANES) + h, peers, stride=pitch), :
                    ] = part[c * peers : (c + 1) * peers, h * LANES : (h + 1) * LANES]
        pack_blocks(wide, stage, send_ref, ssems, pitch)
        for copy in out_copies:
            copy.wait()

    return body


def adapter_body(slots, share, width):
    def body(me_ref, routes_ref, rows_ref, acts_ref, lows_ref, right_ref, *refs):
        shares = refs[:4]
        back_ref = refs[4]
        big, small = refs[5:]
        tokens = routes_ref.shape[1]
        experts = tokens
        down_low = dot(acts_ref[0], right_ref[2], NT).astype(BF16)
        big[0] = SCALE * dot(lows_ref[3], rows_ref[0], TN)
        big[1] = SCALE * dot(lows_ref[4], rows_ref[0], TN)
        big[2] = SCALE * dot(down_low, rows_ref[1], TN)
        small[0] = SCALE * dot(lows_ref[0], acts_ref[1], TN)
        small[1] = SCALE * dot(lows_ref[1], acts_ref[2], TN)
        small[2] = SCALE * dot(lows_ref[2], acts_ref[0], TN)
        for k in range(4):
            at = pl.multiple_of(((me_ref[0] + k) % 4) * width, width)
            for m in range(3):
                shares[k][m, :, 0:width] = big[m, :, pl.ds(at, width)]
                shares[k][m, :, width : width + share] = small[m, :, k * share : (k + 1) * share]
                shares[k][m, :, width + share :] = jnp.zeros((16, 256 - share), F32)
        _, _, either, rank = choice_masks(routes_ref, experts, tokens)
        for c in range(slots):
            back_ref[:, c * experts : (c + 1) * experts] = jnp.where(
                either & (rank == float(c)), 1.0, 0.0
            ).T.astype(BF16)

    return body


def total_body(share, width):
    def body(a_ref, b_ref, c_ref, d_ref, *outs):
        for m in range(3):
            total = a_ref[m] + b_ref[m] + c_ref[m] + d_ref[m]
            outs[m][...] = total[:, :width]
            outs[3 + m][...] = total[:, width : width + share]

    return body


def combine_body(slots):
    def body(back_ref, pick_ref, out_ref, wide, rows):
        experts = back_ref.shape[0]
        _, features = out_ref.shape
        tiles = features // LANES
        depth = slots * tiles

        unpack_blocks(back_ref, wide, depth + 4)
        for j in range(tiles):
            for c in range(slots):
                rows[c * experts : (c + 1) * experts, j * LANES : (j + 1) * LANES] = wide[
                    pl.ds(c * tiles + j, experts, stride=depth + 4), :
                ].astype(BF16)
        for j in range(0, features, 256):
            out_ref[:, j : j + 256] = dot(pick_ref[...], rows[:, j : j + 256]).astype(BF16)

    return body


def layer(
    hidden_in,
    out_grad,
    routes,
    gate_num,
    doc_lengths,
    w_gate,
    w_up,
    w_down,
    a_gate,
    b_gate,
    a_up,
    b_up,
    a_down,
    b_down,
):
    tokens, features = hidden_in.shape[1:]
    groups = lax.axis_size("expert")
    shards = lax.axis_size("dp")
    share = w_gate.shape[1]
    hidden = share * shards
    rank_dim = a_gate.shape[2]
    width = features // shards
    slots = min(tokens, max(2, 3 * tokens * routes.shape[2] // (2 * groups)))
    tiles = features // LANES
    depth = slots * tiles
    rows = slots * groups
    me = lax.axis_index("dp")
    routes_t = routes[0].T
    start = (lax.axis_index("expert") * tokens).astype(jnp.int32).reshape(1)
    x, g = hidden_in[0], out_grad[0]

    up_ring = [(i, (i + 1) % shards) for i in range(shards)]
    down_ring = [(i, (i - 1) % shards) for i in range(shards)]
    (send,) = call(
        dispatch_body(slots, tokens * groups, doc_lengths.shape[1]),
        (*in_hbm((routes_t, gate_num[0].T, doc_lengths)), start, *in_hbm((x, g))),
        [vmem(), vmem(), smem(), smem(), anyspace(), anyspace()],
        [((groups, 2 * depth, LANES), BF16, pltpu.HBM)],
        [anyspace()],
        [
            pltpu.VMEM((groups * (depth + 4), LANES), F32),
            pltpu.VMEM((groups * (depth + 4), LANES), F32),
            pltpu.VMEM((groups, 2 * depth, LANES), BF16),
            pltpu.VMEM((tokens, features), BF16),
            pltpu.VMEM((tokens, features), BF16),
            pltpu.SemaphoreType.DMA((2,)),
            pltpu.SemaphoreType.DMA((2, groups // 8)),
        ],
        4 * rows * tokens * features,
        4 * rows * features,
        16,
    )
    own = (w_gate[0], w_up[0], w_down[0])
    recv = lax.all_to_all(send, "expert", split_axis=0, concat_axis=0, tiled=True)

    half = share // 2
    parts = []
    for w in own:
        behind = lax.ppermute(w, "dp", up_ring)
        ahead = lax.ppermute(w, "dp", down_ring)
        far = [lax.ppermute(behind[:half], "dp", up_ring), lax.ppermute(ahead[half:], "dp", down_ring)]
        parts.append((w, ahead, behind, *far))
    spots = ((0, share), (share, share), (3 * share, share), (2 * share, half), (2 * share + half, half))

    left = jnp.concatenate([a_gate[0].T, a_up[0].T], axis=0)
    right = jnp.stack([b_gate[0], b_up[0], a_down[0].T])
    right = lax.dynamic_slice_in_dim(
        jnp.concatenate([right, right], axis=2), me * share, hidden, axis=2
    )
    row_blocks, s_rows, gates, ups, lows, both = call(
        product_body(slots, [(m, *spot) for m in range(2) for spot in spots]),
        (recv, *in_hbm((*parts[0], *parts[1], left, b_down[0], right))),
        [vmem()] + [anyspace()] * 10 + [vmem()] * 3,
        [
            ((2, rows, features), BF16, pltpu.HBM),
            ((rows, features), BF16, pltpu.VMEM),
            ((rows, hidden), F32, pltpu.VMEM),
            ((rows, hidden), F32, pltpu.VMEM),
            ((3, rows, rank_dim), BF16, pltpu.VMEM),
            ((2, hidden, features), BF16, pltpu.VMEM),
        ],
        [anyspace()] + [vmem()] * 5,
        [
            pltpu.VMEM((rows, features), BF16),
            pltpu.VMEM((groups * (depth + 4), LANES), F32),
            pltpu.VMEM((groups * (tiles + 4), LANES), F32),
            pltpu.SemaphoreType.DMA((10,)),
            pltpu.SemaphoreType.DMA((2,)),
        ],
        4 * rows * hidden * features,
        4 * hidden * features + 4 * rows * features,
        12,
    )
    send_back, acts, all_lows = call(
        expert_body(slots, [(0, *spot) for spot in spots]),
        (*in_vmem((s_rows, gates, ups, lows, both)), *in_hbm((*parts[2], left, right))),
        [vmem()] * 5 + [anyspace()] * 5 + [vmem()] * 2,
        [
            ((groups, depth, LANES), BF16, pltpu.HBM),
            ((3, rows, hidden), BF16, pltpu.HBM),
            ((5, rows, rank_dim), BF16, pltpu.HBM),
        ],
        [anyspace()] * 3,
        [
            pltpu.VMEM((groups * (depth + 4), LANES), F32),
            pltpu.VMEM((1, hidden, features), BF16),
            pltpu.VMEM((3, rows, hidden), BF16),
            pltpu.VMEM((5, rows, rank_dim), BF16),
            pltpu.VMEM((rows, 2 * rank_dim), BF16),
            pltpu.VMEM((groups, depth, LANES), BF16),
            pltpu.SemaphoreType.DMA((5,)),
            pltpu.SemaphoreType.DMA((groups // 8,)),
            pltpu.SemaphoreType.DMA((2,)),
        ],
        6 * rows * hidden * features,
        2 * hidden * features + 2 * rows * features,
        18,
    )
    back = lax.all_to_all(send_back, "expert", split_axis=0, concat_axis=0, tiled=True)

    *shares, pick = call(
        adapter_body(slots, share, width),
        (
            me.astype(jnp.int32).reshape(1),
            *in_hbm((routes_t, row_blocks, acts, all_lows, right)),
        ),
        [smem()] + [vmem()] * 5,
        [((3, rank_dim, width + 256), F32, pltpu.HBM)] * 4 + [((tokens, rows), BF16, pltpu.VMEM)],
        [vmem()] * 5,
        [pltpu.VMEM((3, rank_dim, features), F32), pltpu.VMEM((3, rank_dim, hidden), F32)],
        12 * rows * features * rank_dim,
        4 * rows * features,
        12,
    )
    pieces = [shares[0]] + [
        lax.ppermute(shares[k], "dp", [(i, (i + k) % shards) for i in range(shards)])
        for k in range(1, shards)
    ]
    big_gate, big_up, big_down, small_gate, small_up, small_down = call(
        total_body(share, width),
        pieces,
        [vmem()] * 4,
        [((rank_dim, width), F32, pltpu.HBM)] * 3 + [((rank_dim, share), F32, pltpu.HBM)] * 3,
        [vmem()] * 6,
        [],
        9 * rank_dim * (width + share),
        60 * rank_dim * (width + share),
        4,
    )
    (input_grad,) = call(
        combine_body(slots),
        (back, pltpu.with_memory_space_constraint(pick, pltpu.VMEM)),
        [vmem()] * 2,
        [((tokens, features), BF16, pltpu.HBM)],
        [vmem()],
        [pltpu.VMEM((groups * (depth + 4), LANES), F32), pltpu.VMEM((rows, features), BF16)],
        2 * rows * tokens * features,
        2 * rows * features,
        12,
    )
    return (
        input_grad[None],
        big_gate.T[None],
        small_gate[None],
        big_up.T[None],
        small_up[None],
        small_down.T[None],
        big_down[None],
    )


def solution(mesh):
    return jax.shard_map(
        layer,
        mesh=mesh,
        in_specs=(
            P("dp", "expert", None),
            P("dp", "expert", None),
            P("dp", "expert", None),
            P("dp", "expert", None),
            P("dp", None),
            P("expert", "dp", None),
            P("expert", "dp", None),
            P("expert", "dp", None),
            P("expert", None, None),
            P("expert", None, None),
            P("expert", None, None),
            P("expert", None, None),
            P("expert", None, None),
            P("expert", None, None),
        ),
        out_specs=(
            P("dp", "expert", None),
            P("expert", "dp", None),
            P("expert", None, "dp"),
            P("expert", "dp", None),
            P("expert", None, "dp"),
            P("expert", "dp", None),
            P("expert", None, "dp"),
        ),
        check_vma=False,
    )
```

```python
import jax
import jax.numpy as jnp
from jax import lax
from jax.experimental import pallas as pl
from jax.experimental.pallas import tpu as pltpu
from jax.sharding import PartitionSpec as P


SCALE = 2.0
F32 = jnp.float32
BF16 = jnp.bfloat16
LANES = 128

NN = (((1,), (0,)), ((), ()))
NT = (((1,), (1,)), ((), ()))
TN = (((0,), (0,)), ((), ()))


def dot(left, right, dims=NN):
    return lax.dot_general(left, right, dims, preferred_element_type=F32)


def vmem():
    return pl.BlockSpec(memory_space=pltpu.VMEM)


def in_hbm(arrays):
    return [pltpu.with_memory_space_constraint(a, pltpu.HBM) for a in arrays]


def in_vmem(arrays):
    return [pltpu.with_memory_space_constraint(a, pltpu.VMEM) for a in arrays]


def smem():
    return pl.BlockSpec(memory_space=pltpu.SMEM)


def anyspace():
    return pl.BlockSpec(memory_space=pl.ANY)


def call(body, ins, in_specs, outs, out_specs, scratch, flops, nbytes, mib):
    return pl.pallas_call(
        body,
        out_shape=[space(s, d) for s, d, space in outs],
        in_specs=in_specs,
        out_specs=out_specs,
        scratch_shapes=scratch,
        compiler_params=pltpu.CompilerParams(vmem_limit_bytes=mib * 1024 * 1024),
        cost_estimate=pl.CostEstimate(flops=flops, bytes_accessed=nbytes, transcendentals=0),
    )(*ins)


def pack_blocks(wide, stage, out_ref, sems, pitch):
    blocks, depth, _ = stage.shape

    def copy_of(i):
        some = pl.ds(i * 8, 8)
        return pltpu.make_async_copy(stage.at[some], out_ref.at[some], sems.at[i])

    @pl.loop(0, blocks // 8)
    def _(i):
        for e in range(8):
            at = pl.multiple_of(i * 8 * pitch, 8) + e * pitch
            stage[i * 8 + e] = wide[pl.ds(at, depth), :].astype(BF16)
        copy_of(i).start()

    @pl.loop(0, blocks // 8)
    def _(i):
        copy_of(i).wait()


def unpack_blocks(in_ref, wide, pitch):
    blocks, depth, _ = in_ref.shape

    @pl.loop(0, blocks // 8)
    def _(i):
        for e in range(8):
            at = pl.multiple_of(i * 8 * pitch, 8) + e * pitch
            wide[pl.ds(at, depth), :] = in_ref[i * 8 + e].astype(F32)


def choice_masks(routes_ref, experts, tokens):
    expert_id = lax.broadcasted_iota(jnp.int32, (experts, tokens), 0)
    first = routes_ref[0:1, :] == expert_id
    second = routes_ref[1:2, :] == expert_id
    either = first | second
    earlier = lax.broadcasted_iota(jnp.int32, (tokens, tokens), 0) < lax.broadcasted_iota(
        jnp.int32, (tokens, tokens), 1
    )
    rank = dot(jnp.where(either, 1.0, 0.0).astype(BF16), jnp.where(earlier, 1.0, 0.0).astype(BF16))
    return first, second, either, rank


def dispatch_body(slots, group_tokens, doc_count):
    def body(routes_ref, nums_ref, lengths_ref, start_ref, x_hbm, g_hbm, send_ref, wide, more, stage, x_ref, g_ref, lsems, sems):
        loads = [
            pltpu.make_async_copy(x_hbm, x_ref, lsems.at[0]),
            pltpu.make_async_copy(g_hbm, g_ref, lsems.at[1]),
        ]
        for load in loads:
            load.start()
        experts = stage.shape[0]
        tokens, features = x_ref.shape
        tiles = features // LANES
        depth = slots * tiles
        pitch = depth + 4
        first, second, either, rank = choice_masks(routes_ref, experts, tokens)
        position = start_ref[0] + lax.broadcasted_iota(jnp.int32, (1, tokens), 1)
        own = jnp.zeros((1, tokens), jnp.int32)
        begin = jnp.int32(0)
        for j in range(doc_count):
            length = lengths_ref[0, j]
            own = jnp.where((position >= begin) & (position < begin + length), length, own)
            begin = begin + length
        weight = jnp.sqrt(jnp.float32(group_tokens) / (doc_count * own).astype(F32))
        factor = nums_ref[...].astype(F32) / 1024.0 * weight
        factors = jnp.where(first, factor[0:1, :], 0.0) + jnp.where(second, factor[1:2, :], 0.0)
        picks, scales = [], []
        for c in range(slots):
            chosen = jnp.where(either & (rank == float(c)), 1.0, 0.0)
            scales.append(jnp.sum(chosen * factors, axis=1, keepdims=True))
            picks.append(chosen.astype(BF16))
        pick = jnp.concatenate(picks, axis=0)
        scale = jnp.concatenate(scales, axis=0)
        chunk = 2 * LANES
        copies = []
        for side, (source, scratch) in enumerate(((x_ref, wide), (g_ref, more))):
            loads[side].wait()
            for j in range(features // chunk):
                part = dot(pick, source[:, j * chunk : (j + 1) * chunk])
                if side == 1:
                    part = scale * part
                for c in range(slots):
                    for h in range(2):
                        scratch[pl.ds(c * tiles + 2 * j + h, experts, stride=pitch), :] = part[
                            c * experts : (c + 1) * experts, h * LANES : (h + 1) * LANES
                        ]
            at = pl.ds(side * depth, depth)
            for i in range(experts // 8):
                for e in range(i * 8, i * 8 + 8):
                    stage[e, at, :] = scratch[e * pitch : e * pitch + depth, :].astype(BF16)
                some = pl.ds(i * 8, 8)
                copies.append(
                    pltpu.make_async_copy(
                        stage.at[some, at], send_ref.at[some, at], sems.at[side, i]
                    )
                )
                copies[-1].start()
        for copy in copies:
            copy.wait()

    return body


def product_body(slots, places):
    def body(recv_ref, *refs):
        weight_refs, refs = refs[: len(places)], refs[len(places) :]
        left_ref, bdown_ref, right_ref, rows_out, s, gates, ups, lows_ref, weights, down = refs[:10]
        x, wide, more, sems, osems = refs[10:]
        peers = recv_ref.shape[0]
        features = x.shape[1]
        hidden = gates.shape[1]
        tiles = features // LANES
        depth = slots * tiles
        pitch = depth + 4
        narrow = tiles + 4
        copies = [[], [], []]
        for k, (ref, (m, at, size)) in enumerate(zip(weight_refs, places)):
            to = weights.at[m] if m < 2 else down
            copies[m].append(pltpu.make_async_copy(ref, to.at[pl.ds(at, size)], sems.at[k]))
        for copy in copies[0]:
            copy.start()
        for e in range(peers):
            wide[e * pitch : e * pitch + depth, :] = recv_ref[e, :depth, :].astype(F32)
        for j in range(tiles):
            for c in range(slots):
                x[c * peers : (c + 1) * peers, j * LANES : (j + 1) * LANES] = wide[
                    pl.ds(c * tiles + j, peers, stride=pitch), :
                ].astype(BF16)
        chunk = hidden // slots
        lows = dot(x[...], left_ref[...], NT)
        lows_ref[0] = lows[:, :16].astype(BF16)
        lows_ref[1] = lows[:, 16:].astype(BF16)
        for copy in copies[0]:
            copy.wait()
        for copy in copies[1]:
            copy.start()

        @pl.loop(0, slots)
        def _(c):
            cols = pl.ds(pl.multiple_of(c * chunk, chunk), chunk)
            gates[:, cols] = dot(x[...], weights[0, cols, :], NT) + SCALE * dot(
                lows_ref[0], right_ref[0, :, cols]
            )
            from_row = pl.multiple_of(depth + c * tiles, tiles)
            for e in range(peers):
                more[e * narrow : e * narrow + tiles, :] = recv_ref[e, pl.ds(from_row, tiles), :].astype(F32)
            for j in range(tiles):
                s[pl.ds(pl.multiple_of(c * peers, peers), peers), j * LANES : (j + 1) * LANES] = more[
                    pl.ds(j, peers, stride=narrow), :
                ].astype(BF16)

        for copy in copies[1]:
            copy.wait()
        out_copies = [
            pltpu.make_async_copy(x, rows_out.at[0], osems.at[0]),
            pltpu.make_async_copy(s, rows_out.at[1], osems.at[1]),
        ]
        for copy in copies[2] + out_copies:
            copy.start()
        for n in range(slots):
            cols = slice(n * chunk, (n + 1) * chunk)
            ups[:, cols] = dot(x[...], weights[1, cols, :], NT) + SCALE * dot(
                lows_ref[1], right_ref[1, :, cols]
            )
        lows_ref[2] = dot(s[...], bdown_ref[...], NT).astype(BF16)
        for copy in copies[2] + out_copies:
            copy.wait()

    return body


def expert_body(slots):
    def body(s, gates, ups, lows_ref, weights, near, *refs):
        far_refs, left_ref, right_ref, send_ref, acts_out, lows_out = refs[:2], *refs[2:7]
        wide, far, acts, all_lows, backs, stage, sems, ssems, osems = refs[7:]
        rows, features = s.shape
        hidden = gates.shape[1]
        peers = rows // slots
        tiles = features // LANES
        pitch = slots * tiles + 4
        chunk = 2 * LANES
        half = far_refs[0].shape[0]
        held = near.shape[0] // chunk * chunk
        keep = near.shape[0] - held
        copies = [pltpu.make_async_copy(near.at[pl.ds(held, keep)], far.at[pl.ds(0, keep)], sems.at[2])]
        for k in range(2):
            copies.append(
                pltpu.make_async_copy(far_refs[k], far.at[pl.ds(keep + k * half, half)], sems.at[k])
            )
        for copy in copies:
            copy.start()
        for n in range(hidden // chunk):
            cols = slice(n * chunk, (n + 1) * chunk)
            gate, up = gates[:, cols], ups[:, cols]
            if (n + 1) * chunk <= held:
                down = near[cols, :]
            else:
                for copy in copies:
                    copy.wait()
                down = far[...]
            back = dot(s[...], down, NT) + SCALE * dot(lows_ref[2], right_ref[2, :, cols])
            sigma = jax.nn.sigmoid(gate)
            active = gate * sigma
            acts[0, :, cols] = (active * up).astype(BF16)
            acts[1, :, cols] = (back * up * sigma * (1.0 + gate * (1.0 - sigma))).astype(BF16)
            acts[2, :, cols] = (back * active).astype(BF16)
        gate_back = dot(acts[1], right_ref[0], NT).astype(BF16)
        up_back = dot(acts[2], right_ref[1], NT).astype(BF16)
        all_lows[0:3] = lows_ref[...]
        all_lows[3] = gate_back
        all_lows[4] = up_back
        out_copies = [
            pltpu.make_async_copy(acts, acts_out, osems.at[0]),
            pltpu.make_async_copy(all_lows, lows_out, osems.at[1]),
        ]
        for copy in out_copies:
            copy.start()
        backs[:, :16] = gate_back
        backs[:, 16:] = up_back
        for j in range(features // chunk):
            cols = slice(j * chunk, (j + 1) * chunk)
            part = (
                dot(acts[1], weights[0, :, cols])
                + dot(acts[2], weights[1, :, cols])
                + SCALE * dot(backs[...], left_ref[:, cols])
            )
            for c in range(slots):
                for h in range(chunk // LANES):
                    wide[
                        pl.ds(c * tiles + j * (chunk // LANES) + h, peers, stride=pitch), :
                    ] = part[c * peers : (c + 1) * peers, h * LANES : (h + 1) * LANES]
        pack_blocks(wide, stage, send_ref, ssems, pitch)
        for copy in out_copies:
            copy.wait()

    return body


def adapter_body(slots, share, width):
    def body(me_ref, routes_ref, rows_ref, acts_ref, lows_ref, right_ref, *refs):
        shares = refs[:4]
        back_ref = refs[4]
        big, small = refs[5:]
        tokens = routes_ref.shape[1]
        experts = tokens
        down_low = dot(acts_ref[0], right_ref[2], NT).astype(BF16)
        big[0] = SCALE * dot(lows_ref[3], rows_ref[0], TN)
        big[1] = SCALE * dot(lows_ref[4], rows_ref[0], TN)
        big[2] = SCALE * dot(down_low, rows_ref[1], TN)
        small[0] = SCALE * dot(lows_ref[0], acts_ref[1], TN)
        small[1] = SCALE * dot(lows_ref[1], acts_ref[2], TN)
        small[2] = SCALE * dot(lows_ref[2], acts_ref[0], TN)
        for k in range(4):
            at = pl.multiple_of(((me_ref[0] + k) % 4) * width, width)
            for m in range(3):
                shares[k][m, :, 0:width] = big[m, :, pl.ds(at, width)]
                shares[k][m, :, width : width + share] = small[m, :, (k + 1) % 4 * share : ((k + 1) % 4 + 1) * share]
                shares[k][m, :, width + share :] = jnp.zeros((16, 256 - share), F32)
        _, _, either, rank = choice_masks(routes_ref, experts, tokens)
        for c in range(slots):
            back_ref[:, c * experts : (c + 1) * experts] = jnp.where(
                either & (rank == float(c)), 1.0, 0.0
            ).T.astype(BF16)

    return body


def total_body(share, width):
    def body(a_ref, b_ref, c_ref, d_ref, *outs):
        for m in range(3):
            total = a_ref[m] + b_ref[m] + c_ref[m] + d_ref[m]
            outs[m][...] = total[:, :width]
            outs[3 + m][...] = total[:, width : width + share]

    return body


def combine_body(slots):
    def body(back_ref, pick_ref, out_ref, wide, rows):
        experts = back_ref.shape[0]
        _, features = out_ref.shape
        tiles = features // LANES
        depth = slots * tiles

        unpack_blocks(back_ref, wide, depth + 4)
        for j in range(tiles):
            for c in range(slots):
                rows[c * experts : (c + 1) * experts, j * LANES : (j + 1) * LANES] = wide[
                    pl.ds(c * tiles + j, experts, stride=depth + 4), :
                ].astype(BF16)
        for j in range(0, features, 256):
            out_ref[:, j : j + 256] = dot(pick_ref[...], rows[:, j : j + 256]).astype(BF16)

    return body


def layer(
    hidden_in,
    out_grad,
    routes,
    gate_num,
    doc_lengths,
    w_gate,
    w_up,
    w_down,
    a_gate,
    b_gate,
    a_up,
    b_up,
    a_down,
    b_down,
):
    tokens, features = hidden_in.shape[1:]
    groups = lax.axis_size("expert")
    shards = lax.axis_size("dp")
    share = w_gate.shape[1]
    hidden = share * shards
    rank_dim = a_gate.shape[2]
    width = features // shards
    slots = min(tokens, max(2, 3 * tokens * routes.shape[2] // (2 * groups)))
    tiles = features // LANES
    depth = slots * tiles
    rows = slots * groups
    me = lax.axis_index("dp")
    routes_t = routes[0].T
    start = (lax.axis_index("expert") * tokens).astype(jnp.int32).reshape(1)
    x, g = hidden_in[0], out_grad[0]

    up_ring = [(i, (i + 1) % shards) for i in range(shards)]
    down_ring = [(i, (i - 1) % shards) for i in range(shards)]
    (send,) = call(
        dispatch_body(slots, tokens * groups, doc_lengths.shape[1]),
        (*in_hbm((routes_t, gate_num[0].T, doc_lengths)), start, *in_hbm((x, g))),
        [vmem(), vmem(), smem(), smem(), anyspace(), anyspace()],
        [((groups, 2 * depth, LANES), BF16, pltpu.HBM)],
        [anyspace()],
        [
            pltpu.VMEM((groups * (depth + 4), LANES), F32),
            pltpu.VMEM((groups * (depth + 4), LANES), F32),
            pltpu.VMEM((groups, 2 * depth, LANES), BF16),
            pltpu.VMEM((tokens, features), BF16),
            pltpu.VMEM((tokens, features), BF16),
            pltpu.SemaphoreType.DMA((2,)),
            pltpu.SemaphoreType.DMA((2, groups // 8)),
        ],
        4 * rows * tokens * features,
        4 * rows * features,
        16,
    )
    own = (w_gate[0], w_up[0], w_down[0])
    recv = lax.all_to_all(send, "expert", split_axis=0, concat_axis=0, tiled=True)

    half = share // 2
    parts = []
    for w in own:
        behind = lax.ppermute(w, "dp", up_ring)
        ahead = lax.ppermute(w, "dp", down_ring)
        far = [lax.ppermute(behind[:half], "dp", up_ring), lax.ppermute(ahead[half:], "dp", down_ring)]
        parts.append((w, ahead, behind, *far))
    spots = ((share, share), (2 * share, share), (0, share), (3 * share, half), (3 * share + half, half))
    near = spots[:3]

    left = jnp.concatenate([a_gate[0].T, a_up[0].T], axis=0)
    right = jnp.stack([b_gate[0], b_up[0], a_down[0].T])
    right = lax.dynamic_slice_in_dim(
        jnp.concatenate([right, right], axis=2), (me + shards - 1) % shards * share, hidden, axis=2
    )
    row_blocks, s_rows, gates, ups, lows, both, near_down = call(
        product_body(
            slots,
            [(m, *spot) for m in range(2) for spot in spots] + [(2, *spot) for spot in near],
        ),
        (recv, *in_hbm((*parts[0], *parts[1], *parts[2][:3])), *in_vmem((left, b_down[0], right))),
        [vmem()] + [anyspace()] * 13 + [vmem()] * 3,
        [
            ((2, rows, features), BF16, pltpu.HBM),
            ((rows, features), BF16, pltpu.VMEM),
            ((rows, hidden), F32, pltpu.VMEM),
            ((rows, hidden), F32, pltpu.VMEM),
            ((3, rows, rank_dim), BF16, pltpu.VMEM),
            ((2, hidden, features), BF16, pltpu.VMEM),
            ((3 * share, features), BF16, pltpu.VMEM),
        ],
        [anyspace()] + [vmem()] * 6,
        [
            pltpu.VMEM((rows, features), BF16),
            pltpu.VMEM((groups * (depth + 4), LANES), F32),
            pltpu.VMEM((groups * (tiles + 4), LANES), F32),
            pltpu.SemaphoreType.DMA((13,)),
            pltpu.SemaphoreType.DMA((2,)),
        ],
        4 * rows * hidden * features,
        4 * hidden * features + 4 * rows * features,
        12,
    )
    send_back, acts, all_lows = call(
        expert_body(slots),
        (
            *in_vmem((s_rows, gates, ups, lows, both, near_down)),
            *in_hbm(parts[2][3:]),
            *in_vmem((left, right)),
        ),
        [vmem()] * 6 + [anyspace()] * 2 + [vmem()] * 2,
        [
            ((groups, depth, LANES), BF16, pltpu.HBM),
            ((3, rows, hidden), BF16, pltpu.HBM),
            ((5, rows, rank_dim), BF16, pltpu.HBM),
        ],
        [anyspace()] * 3,
        [
            pltpu.VMEM((groups * (depth + 4), LANES), F32),
            pltpu.VMEM((2 * LANES, features), BF16),
            pltpu.VMEM((3, rows, hidden), BF16),
            pltpu.VMEM((5, rows, rank_dim), BF16),
            pltpu.VMEM((rows, 2 * rank_dim), BF16),
            pltpu.VMEM((groups, depth, LANES), BF16),
            pltpu.SemaphoreType.DMA((3,)),
            pltpu.SemaphoreType.DMA((groups // 8,)),
            pltpu.SemaphoreType.DMA((2,)),
        ],
        6 * rows * hidden * features,
        2 * hidden * features + 2 * rows * features,
        18,
    )
    back = lax.all_to_all(send_back, "expert", split_axis=0, concat_axis=0, tiled=True)

    *shares, pick = call(
        adapter_body(slots, share, width),
        (
            me.astype(jnp.int32).reshape(1),
            *in_hbm((routes_t, row_blocks, acts, all_lows, right)),
        ),
        [smem()] + [vmem()] * 5,
        [((3, rank_dim, width + 256), F32, pltpu.HBM)] * 4 + [((tokens, rows), BF16, pltpu.VMEM)],
        [vmem()] * 5,
        [pltpu.VMEM((3, rank_dim, features), F32), pltpu.VMEM((3, rank_dim, hidden), F32)],
        12 * rows * features * rank_dim,
        4 * rows * features,
        12,
    )
    pieces = [shares[0]] + [
        lax.ppermute(shares[k], "dp", [(i, (i + k) % shards) for i in range(shards)])
        for k in range(1, shards)
    ]
    big_gate, big_up, big_down, small_gate, small_up, small_down = call(
        total_body(share, width),
        pieces,
        [vmem()] * 4,
        [((rank_dim, width), F32, pltpu.HBM)] * 3 + [((rank_dim, share), F32, pltpu.HBM)] * 3,
        [vmem()] * 6,
        [],
        9 * rank_dim * (width + share),
        60 * rank_dim * (width + share),
        4,
    )
    (input_grad,) = call(
        combine_body(slots),
        (back, pltpu.with_memory_space_constraint(pick, pltpu.VMEM)),
        [vmem()] * 2,
        [((tokens, features), BF16, pltpu.HBM)],
        [vmem()],
        [pltpu.VMEM((groups * (depth + 4), LANES), F32), pltpu.VMEM((rows, features), BF16)],
        2 * rows * tokens * features,
        2 * rows * features,
        12,
    )
    return (
        input_grad[None],
        big_gate.T[None],
        small_gate[None],
        big_up.T[None],
        small_up[None],
        small_down.T[None],
        big_down[None],
    )


def solution(mesh):
    return jax.shard_map(
        layer,
        mesh=mesh,
        in_specs=(
            P("dp", "expert", None),
            P("dp", "expert", None),
            P("dp", "expert", None),
            P("dp", "expert", None),
            P("dp", None),
            P("expert", "dp", None),
            P("expert", "dp", None),
            P("expert", "dp", None),
            P("expert", None, None),
            P("expert", None, None),
            P("expert", None, None),
            P("expert", None, None),
            P("expert", None, None),
            P("expert", None, None),
        ),
        out_specs=(
            P("dp", "expert", None),
            P("expert", "dp", None),
            P("expert", None, "dp"),
            P("expert", "dp", None),
            P("expert", None, "dp"),
            P("expert", "dp", None),
            P("expert", None, "dp"),
        ),
        check_vma=False,
    )
```

```python
import jax
import jax.numpy as jnp
from jax import lax
from jax.experimental import pallas as pl
from jax.experimental.pallas import tpu as pltpu
from jax.sharding import PartitionSpec as P


SCALE = 2.0
F32 = jnp.float32
BF16 = jnp.bfloat16
LANES = 128

NN = (((1,), (0,)), ((), ()))
NT = (((1,), (1,)), ((), ()))
TN = (((0,), (0,)), ((), ()))


def dot(left, right, dims=NN):
    return lax.dot_general(left, right, dims, preferred_element_type=F32)


def vmem():
    return pl.BlockSpec(memory_space=pltpu.VMEM)


def in_hbm(arrays):
    return [pltpu.with_memory_space_constraint(a, pltpu.HBM) for a in arrays]


def in_vmem(arrays):
    return [pltpu.with_memory_space_constraint(a, pltpu.VMEM) for a in arrays]


def smem():
    return pl.BlockSpec(memory_space=pltpu.SMEM)


def anyspace():
    return pl.BlockSpec(memory_space=pl.ANY)


def call(body, ins, in_specs, outs, out_specs, scratch, flops, nbytes, mib):
    return pl.pallas_call(
        body,
        out_shape=[space(s, d) for s, d, space in outs],
        in_specs=in_specs,
        out_specs=out_specs,
        scratch_shapes=scratch,
        compiler_params=pltpu.CompilerParams(vmem_limit_bytes=mib * 1024 * 1024),
        cost_estimate=pl.CostEstimate(flops=flops, bytes_accessed=nbytes, transcendentals=0),
    )(*ins)


def pack_blocks(wide, stage, out_ref, sems, pitch):
    blocks, depth, _ = stage.shape

    def copy_of(i):
        some = pl.ds(i * 8, 8)
        return pltpu.make_async_copy(stage.at[some], out_ref.at[some], sems.at[i])

    @pl.loop(0, blocks // 8)
    def _(i):
        for e in range(8):
            at = pl.multiple_of(i * 8 * pitch, 8) + e * pitch
            stage[i * 8 + e] = wide[pl.ds(at, depth), :].astype(BF16)
        copy_of(i).start()

    @pl.loop(0, blocks // 8)
    def _(i):
        copy_of(i).wait()


def unpack_blocks(in_ref, wide, pitch):
    blocks, depth, _ = in_ref.shape

    @pl.loop(0, blocks // 8)
    def _(i):
        for e in range(8):
            at = pl.multiple_of(i * 8 * pitch, 8) + e * pitch
            wide[pl.ds(at, depth), :] = in_ref[i * 8 + e].astype(F32)


def choice_masks(routes_ref, experts, tokens):
    expert_id = lax.broadcasted_iota(jnp.int32, (experts, tokens), 0)
    first = routes_ref[0:1, :] == expert_id
    second = routes_ref[1:2, :] == expert_id
    either = first | second
    earlier = lax.broadcasted_iota(jnp.int32, (tokens, tokens), 0) < lax.broadcasted_iota(
        jnp.int32, (tokens, tokens), 1
    )
    rank = dot(jnp.where(either, 1.0, 0.0).astype(BF16), jnp.where(earlier, 1.0, 0.0).astype(BF16))
    return first, second, either, rank


def dispatch_body(slots, group_tokens, doc_count):
    def body(start_ref, x_hbm, g_hbm, routes_hbm, nums_hbm, lengths_hbm, send_ref, *scratches):
        wide, more, stage, x_ref, g_ref, routes_ref, nums_ref, lengths_ref, lsems, sems = scratches
        loads = [
            pltpu.make_async_copy(routes_hbm, routes_ref, lsems.at[0]),
            pltpu.make_async_copy(nums_hbm, nums_ref, lsems.at[1]),
            pltpu.make_async_copy(lengths_hbm, lengths_ref, lsems.at[2]),
            pltpu.make_async_copy(x_hbm, x_ref, lsems.at[3]),
            pltpu.make_async_copy(g_hbm, g_ref, lsems.at[4]),
        ]
        for load in loads:
            load.start()
        for load in loads[:3]:
            load.wait()
        experts = stage.shape[0]
        tokens, features = x_ref.shape
        tiles = features // LANES
        depth = slots * tiles
        pitch = depth + 4
        first, second, either, rank = choice_masks(routes_ref, experts, tokens)
        position = start_ref[0] + lax.broadcasted_iota(jnp.int32, (1, tokens), 1)
        own = jnp.zeros((1, tokens), jnp.int32)
        begin = jnp.int32(0)
        for j in range(doc_count):
            length = lengths_ref[0, j]
            own = jnp.where((position >= begin) & (position < begin + length), length, own)
            begin = begin + length
        weight = jnp.sqrt(jnp.float32(group_tokens) / (doc_count * own).astype(F32))
        factor = nums_ref[...].astype(F32) / 1024.0 * weight
        factors = jnp.where(first, factor[0:1, :], 0.0) + jnp.where(second, factor[1:2, :], 0.0)
        picks, scales = [], []
        for c in range(slots):
            chosen = jnp.where(either & (rank == float(c)), 1.0, 0.0)
            scales.append(jnp.sum(chosen * factors, axis=1, keepdims=True))
            picks.append(chosen.astype(BF16))
        pick = jnp.concatenate(picks, axis=0)
        scale = jnp.concatenate(scales, axis=0)
        chunk = 2 * LANES
        copies = []
        for side, (source, scratch) in enumerate(((x_ref, wide), (g_ref, more))):
            loads[3 + side].wait()
            for j in range(features // chunk):
                part = dot(pick, source[:, j * chunk : (j + 1) * chunk])
                if side == 1:
                    part = scale * part
                for c in range(slots):
                    for h in range(2):
                        scratch[pl.ds(c * tiles + 2 * j + h, experts, stride=pitch), :] = part[
                            c * experts : (c + 1) * experts, h * LANES : (h + 1) * LANES
                        ]
            at = pl.ds(side * depth, depth)
            for i in range(experts // 8):
                for e in range(i * 8, i * 8 + 8):
                    stage[e, at, :] = scratch[e * pitch : e * pitch + depth, :].astype(BF16)
                some = pl.ds(i * 8, 8)
                copies.append(
                    pltpu.make_async_copy(
                        stage.at[some, at], send_ref.at[some, at], sems.at[side, i]
                    )
                )
                copies[-1].start()
        for copy in copies:
            copy.wait()

    return body


def product_body(slots, places):
    def body(recv_ref, *refs):
        weight_refs, refs = refs[: len(places)], refs[len(places) :]
        left_ref, bdown_ref, right_ref, rows_out, s, gates, ups, lows_ref, weights, down = refs[:10]
        x, wide, more, sems, osems = refs[10:]
        peers = recv_ref.shape[0]
        features = x.shape[1]
        hidden = gates.shape[1]
        tiles = features // LANES
        depth = slots * tiles
        pitch = depth + 4
        copies = [[], [], []]
        for k, (ref, (m, at, size)) in enumerate(zip(weight_refs, places)):
            to = weights.at[m] if m < 2 else down
            copies[m].append(pltpu.make_async_copy(ref, to.at[pl.ds(at, size)], sems.at[k]))
        for copy in copies[0]:
            copy.start()
        for side, (scratch, rows) in enumerate(((wide, x), (more, s))):
            for e in range(peers):
                scratch[e * pitch : e * pitch + depth, :] = recv_ref[
                    e, side * depth : (side + 1) * depth, :
                ].astype(F32)
            for j in range(tiles):
                for c in range(slots):
                    rows[c * peers : (c + 1) * peers, j * LANES : (j + 1) * LANES] = scratch[
                        pl.ds(c * tiles + j, peers, stride=pitch), :
                    ].astype(BF16)
        lows = dot(x[...], left_ref[...], NT)
        lows_ref[0] = lows[:, :16].astype(BF16)
        lows_ref[1] = lows[:, 16:].astype(BF16)
        lows_ref[2] = dot(s[...], bdown_ref[...], NT).astype(BF16)
        chunk = 2 * LANES
        for copy in copies[0]:
            copy.wait()
        for copy in copies[1]:
            copy.start()
        for n in range(hidden // chunk):
            cols = slice(n * chunk, (n + 1) * chunk)
            gates[:, cols] = dot(x[...], weights[0, cols, :], NT) + SCALE * dot(
                lows_ref[0], right_ref[0, :, cols]
            )
        for copy in copies[1]:
            copy.wait()
        out_copies = [
            pltpu.make_async_copy(x, rows_out.at[0], osems.at[0]),
            pltpu.make_async_copy(s, rows_out.at[1], osems.at[1]),
        ]
        for copy in copies[2] + out_copies:
            copy.start()
        for n in range(hidden // chunk):
            cols = slice(n * chunk, (n + 1) * chunk)
            ups[:, cols] = dot(x[...], weights[1, cols, :], NT) + SCALE * dot(
                lows_ref[1], right_ref[1, :, cols]
            )
        for copy in copies[2] + out_copies:
            copy.wait()

    return body


def expert_body(slots):
    def body(s, gates, ups, lows_ref, weights, near, *refs):
        far_refs, left_ref, right_ref, send_ref, acts_out, lows_out = refs[:2], *refs[2:7]
        wide, far, acts, all_lows, backs, stage, sems, ssems, osems = refs[7:]
        rows, features = s.shape
        hidden = gates.shape[1]
        peers = rows // slots
        tiles = features // LANES
        pitch = slots * tiles + 4
        chunk = 2 * LANES
        half = far_refs[0].shape[0]
        held = near.shape[0] // chunk * chunk
        keep = near.shape[0] - held
        copies = [pltpu.make_async_copy(near.at[pl.ds(held, keep)], far.at[pl.ds(0, keep)], sems.at[2])]
        for k in range(2):
            copies.append(
                pltpu.make_async_copy(far_refs[k], far.at[pl.ds(keep + k * half, half)], sems.at[k])
            )
        for copy in copies:
            copy.start()
        for n in range(hidden // chunk):
            cols = slice(n * chunk, (n + 1) * chunk)
            gate, up = gates[:, cols], ups[:, cols]
            if (n + 1) * chunk <= held:
                down = near[cols, :]
            else:
                for copy in copies:
                    copy.wait()
                down = far[...]
            back = dot(s[...], down, NT) + SCALE * dot(lows_ref[2], right_ref[2, :, cols])
            sigma = jax.nn.sigmoid(gate)
            active = gate * sigma
            acts[0, :, cols] = (active * up).astype(BF16)
            acts[1, :, cols] = (back * up * sigma * (1.0 + gate * (1.0 - sigma))).astype(BF16)
            acts[2, :, cols] = (back * active).astype(BF16)
        gate_back = dot(acts[1], right_ref[0], NT).astype(BF16)
        up_back = dot(acts[2], right_ref[1], NT).astype(BF16)
        all_lows[0:3] = lows_ref[...]
        all_lows[3] = gate_back
        all_lows[4] = up_back
        out_copies = [
            pltpu.make_async_copy(acts, acts_out, osems.at[0]),
            pltpu.make_async_copy(all_lows, lows_out, osems.at[1]),
        ]
        for copy in out_copies:
            copy.start()
        backs[:, :16] = gate_back
        backs[:, 16:] = up_back
        for j in range(features // chunk):
            cols = slice(j * chunk, (j + 1) * chunk)
            part = (
                dot(acts[1], weights[0, :, cols])
                + dot(acts[2], weights[1, :, cols])
                + SCALE * dot(backs[...], left_ref[:, cols])
            )
            for c in range(slots):
                for h in range(chunk // LANES):
                    wide[
                        pl.ds(c * tiles + j * (chunk // LANES) + h, peers, stride=pitch), :
                    ] = part[c * peers : (c + 1) * peers, h * LANES : (h + 1) * LANES]
        pack_blocks(wide, stage, send_ref, ssems, pitch)
        for copy in out_copies:
            copy.wait()

    return body


def adapter_body(slots, share, width):
    def body(me_ref, routes_ref, rows_ref, acts_ref, lows_ref, right_ref, *refs):
        shares = refs[:4]
        back_ref = refs[4]
        big, small = refs[5:]
        tokens = routes_ref.shape[1]
        experts = tokens
        down_low = dot(acts_ref[0], right_ref[2], NT).astype(BF16)
        big[0] = SCALE * dot(lows_ref[3], rows_ref[0], TN)
        big[1] = SCALE * dot(lows_ref[4], rows_ref[0], TN)
        big[2] = SCALE * dot(down_low, rows_ref[1], TN)
        small[0] = SCALE * dot(lows_ref[0], acts_ref[1], TN)
        small[1] = SCALE * dot(lows_ref[1], acts_ref[2], TN)
        small[2] = SCALE * dot(lows_ref[2], acts_ref[0], TN)
        for k in range(4):
            at = pl.multiple_of(((me_ref[0] + k) % 4) * width, width)
            for m in range(3):
                shares[k][m, :, 0:width] = big[m, :, pl.ds(at, width)]
                shares[k][m, :, width : width + share] = small[m, :, (k + 1) % 4 * share : ((k + 1) % 4 + 1) * share]
                shares[k][m, :, width + share :] = jnp.zeros((16, 256 - share), F32)
        _, _, either, rank = choice_masks(routes_ref, experts, tokens)
        for c in range(slots):
            back_ref[:, c * experts : (c + 1) * experts] = jnp.where(
                either & (rank == float(c)), 1.0, 0.0
            ).T.astype(BF16)

    return body


def total_body(share, width):
    def body(a_ref, b_ref, c_ref, d_ref, *outs):
        for m in range(3):
            total = a_ref[m] + b_ref[m] + c_ref[m] + d_ref[m]
            outs[m][...] = total[:, :width]
            outs[3 + m][...] = total[:, width : width + share]

    return body


def combine_body(slots):
    def body(back_ref, pick_ref, out_ref, wide, rows):
        experts = back_ref.shape[0]
        _, features = out_ref.shape
        tiles = features // LANES
        depth = slots * tiles

        unpack_blocks(back_ref, wide, depth + 4)
        for j in range(tiles):
            for c in range(slots):
                rows[c * experts : (c + 1) * experts, j * LANES : (j + 1) * LANES] = wide[
                    pl.ds(c * tiles + j, experts, stride=depth + 4), :
                ].astype(BF16)
        for j in range(0, features, 256):
            out_ref[:, j : j + 256] = dot(pick_ref[...], rows[:, j : j + 256]).astype(BF16)

    return body


def layer(
    hidden_in,
    out_grad,
    routes,
    gate_num,
    doc_lengths,
    w_gate,
    w_up,
    w_down,
    a_gate,
    b_gate,
    a_up,
    b_up,
    a_down,
    b_down,
):
    tokens, features = hidden_in.shape[1:]
    groups = lax.axis_size("expert")
    shards = lax.axis_size("dp")
    share = w_gate.shape[1]
    hidden = share * shards
    rank_dim = a_gate.shape[2]
    width = features // shards
    slots = min(tokens, max(2, 3 * tokens * routes.shape[2] // (2 * groups)))
    tiles = features // LANES
    depth = slots * tiles
    rows = slots * groups
    me = lax.axis_index("dp")
    routes_t = routes[0].T
    start = (lax.axis_index("expert") * tokens).astype(jnp.int32).reshape(1)
    x, g = hidden_in[0], out_grad[0]

    up_ring = [(i, (i + 1) % shards) for i in range(shards)]
    down_ring = [(i, (i - 1) % shards) for i in range(shards)]
    (send,) = call(
        dispatch_body(slots, tokens * groups, doc_lengths.shape[1]),
        (start, *in_hbm((x, g, routes_t, gate_num[0].T, doc_lengths))),
        [smem()] + [anyspace()] * 5,
        [((groups, 2 * depth, LANES), BF16, pltpu.HBM)],
        [anyspace()],
        [
            pltpu.VMEM((groups * (depth + 4), LANES), F32),
            pltpu.VMEM((groups * (depth + 4), LANES), F32),
            pltpu.VMEM((groups, 2 * depth, LANES), BF16),
            pltpu.VMEM((tokens, features), BF16),
            pltpu.VMEM((tokens, features), BF16),
            pltpu.VMEM(routes_t.shape, jnp.int32),
            pltpu.VMEM(routes_t.shape, jnp.int32),
            pltpu.SMEM(doc_lengths.shape, jnp.int32),
            pltpu.SemaphoreType.DMA((5,)),
            pltpu.SemaphoreType.DMA((2, groups // 8)),
        ],
        4 * rows * tokens * features,
        4 * rows * features,
        16,
    )
    own = (w_gate[0], w_up[0], w_down[0])
    recv = lax.all_to_all(send, "expert", split_axis=0, concat_axis=0, tiled=True)

    half = share // 2
    parts = []
    for w, name in zip(own, ("gatering", "upring", "lastring")):
        behind = lax.ppermute(w, "dp", up_ring)
        ahead = lax.ppermute(w, "dp", down_ring)
        if name == "gatering":
            far = [lax.ppermute(ahead, "dp", down_ring)]
        elif name == "upring":
            far = [lax.ppermute(behind, "dp", up_ring)]
        else:
            far = [lax.ppermute(behind[:half], "dp", up_ring), lax.ppermute(ahead[half:], "dp", down_ring)]
        parts.append((w, ahead, behind, *far))
    near = ((share, share), (2 * share, share), (0, share))
    spots = (*near, (3 * share, share))

    left = jnp.concatenate([a_gate[0].T, a_up[0].T], axis=0)
    right = jnp.stack([b_gate[0], b_up[0], a_down[0].T])
    right = lax.dynamic_slice_in_dim(
        jnp.concatenate([right, right], axis=2), (me + shards - 1) % shards * share, hidden, axis=2
    )
    row_blocks, s_rows, gates, ups, lows, both, near_down = call(
        product_body(
            slots,
            [(m, *spot) for m in range(2) for spot in spots] + [(2, *spot) for spot in near],
        ),
        (recv, *in_hbm((*parts[0], *parts[1], *parts[2][:3])), *in_vmem((left, b_down[0], right))),
        [vmem()] + [anyspace()] * 11 + [vmem()] * 3,
        [
            ((2, rows, features), BF16, pltpu.HBM),
            ((rows, features), BF16, pltpu.VMEM),
            ((rows, hidden), F32, pltpu.VMEM),
            ((rows, hidden), F32, pltpu.VMEM),
            ((3, rows, rank_dim), BF16, pltpu.VMEM),
            ((2, hidden, features), BF16, pltpu.VMEM),
            ((3 * share, features), BF16, pltpu.VMEM),
        ],
        [anyspace()] + [vmem()] * 6,
        [
            pltpu.VMEM((rows, features), BF16),
            pltpu.VMEM((groups * (depth + 4), LANES), F32),
            pltpu.VMEM((groups * (depth + 4), LANES), F32),
            pltpu.SemaphoreType.DMA((11,)),
            pltpu.SemaphoreType.DMA((2,)),
        ],
        4 * rows * hidden * features,
        4 * hidden * features + 4 * rows * features,
        14,
    )
    send_back, acts, all_lows = call(
        expert_body(slots),
        (
            *in_vmem((s_rows, gates, ups, lows, both, near_down)),
            *in_hbm(parts[2][3:]),
            *in_vmem((left, right)),
        ),
        [vmem()] * 6 + [anyspace()] * 2 + [vmem()] * 2,
        [
            ((groups, depth, LANES), BF16, pltpu.HBM),
            ((3, rows, hidden), BF16, pltpu.HBM),
            ((5, rows, rank_dim), BF16, pltpu.HBM),
        ],
        [anyspace()] * 3,
        [
            pltpu.VMEM((groups * (depth + 4), LANES), F32),
            pltpu.VMEM((2 * LANES, features), BF16),
            pltpu.VMEM((3, rows, hidden), BF16),
            pltpu.VMEM((5, rows, rank_dim), BF16),
            pltpu.VMEM((rows, 2 * rank_dim), BF16),
            pltpu.VMEM((groups, depth, LANES), BF16),
            pltpu.SemaphoreType.DMA((3,)),
            pltpu.SemaphoreType.DMA((groups // 8,)),
            pltpu.SemaphoreType.DMA((2,)),
        ],
        6 * rows * hidden * features,
        2 * hidden * features + 2 * rows * features,
        18,
    )
    back = lax.all_to_all(send_back, "expert", split_axis=0, concat_axis=0, tiled=True)

    *shares, pick = call(
        adapter_body(slots, share, width),
        (
            me.astype(jnp.int32).reshape(1),
            *in_hbm((routes_t, row_blocks, acts, all_lows, right)),
        ),
        [smem()] + [vmem()] * 5,
        [((3, rank_dim, width + 256), F32, pltpu.HBM)] * 4 + [((tokens, rows), BF16, pltpu.VMEM)],
        [vmem()] * 5,
        [pltpu.VMEM((3, rank_dim, features), F32), pltpu.VMEM((3, rank_dim, hidden), F32)],
        12 * rows * features * rank_dim,
        4 * rows * features,
        12,
    )
    pieces = [shares[0]] + [
        lax.ppermute(shares[k], "dp", [(i, (i + k) % shards) for i in range(shards)])
        for k in range(1, shards)
    ]
    big_gate, big_up, big_down, small_gate, small_up, small_down = call(
        total_body(share, width),
        pieces,
        [vmem()] * 4,
        [((rank_dim, width), F32, pltpu.HBM)] * 3 + [((rank_dim, share), F32, pltpu.HBM)] * 3,
        [vmem()] * 6,
        [],
        9 * rank_dim * (width + share),
        60 * rank_dim * (width + share),
        4,
    )
    (input_grad,) = call(
        combine_body(slots),
        (back, pltpu.with_memory_space_constraint(pick, pltpu.VMEM)),
        [vmem()] * 2,
        [((tokens, features), BF16, pltpu.HBM)],
        [vmem()],
        [pltpu.VMEM((groups * (depth + 4), LANES), F32), pltpu.VMEM((rows, features), BF16)],
        2 * rows * tokens * features,
        2 * rows * features,
        12,
    )
    return (
        input_grad[None],
        big_gate.T[None],
        small_gate[None],
        big_up.T[None],
        small_up[None],
        small_down.T[None],
        big_down[None],
    )


def solution(mesh):
    return jax.shard_map(
        layer,
        mesh=mesh,
        in_specs=(
            P("dp", "expert", None),
            P("dp", "expert", None),
            P("dp", "expert", None),
            P("dp", "expert", None),
            P("dp", None),
            P("expert", "dp", None),
            P("expert", "dp", None),
            P("expert", "dp", None),
            P("expert", None, None),
            P("expert", None, None),
            P("expert", None, None),
            P("expert", None, None),
            P("expert", None, None),
            P("expert", None, None),
        ),
        out_specs=(
            P("dp", "expert", None),
            P("expert", "dp", None),
            P("expert", None, "dp"),
            P("expert", "dp", None),
            P("expert", None, "dp"),
            P("expert", "dp", None),
            P("expert", None, "dp"),
        ),
        check_vma=False,
    )
```

```python
import jax
import jax.numpy as jnp
from jax import lax
from jax.experimental import pallas as pl
from jax.experimental.pallas import tpu as pltpu
from jax.sharding import PartitionSpec as P


SCALE = 2.0
F32 = jnp.float32
BF16 = jnp.bfloat16
LANES = 128

NN = (((1,), (0,)), ((), ()))
NT = (((1,), (1,)), ((), ()))
TN = (((0,), (0,)), ((), ()))


def dot(left, right, dims=NN):
    return lax.dot_general(left, right, dims, preferred_element_type=F32)


def vmem():
    return pl.BlockSpec(memory_space=pltpu.VMEM)


def in_hbm(arrays):
    return [pltpu.with_memory_space_constraint(a, pltpu.HBM) for a in arrays]


def in_vmem(arrays):
    return [pltpu.with_memory_space_constraint(a, pltpu.VMEM) for a in arrays]


def smem():
    return pl.BlockSpec(memory_space=pltpu.SMEM)


def anyspace():
    return pl.BlockSpec(memory_space=pl.ANY)


def call(body, ins, in_specs, outs, out_specs, scratch, flops, nbytes, mib):
    return pl.pallas_call(
        body,
        out_shape=[space(s, d) for s, d, space in outs],
        in_specs=in_specs,
        out_specs=out_specs,
        scratch_shapes=scratch,
        compiler_params=pltpu.CompilerParams(vmem_limit_bytes=mib * 1024 * 1024),
        cost_estimate=pl.CostEstimate(flops=flops, bytes_accessed=nbytes, transcendentals=0),
    )(*ins)


def pack_blocks(wide, stage, out_ref, sems, pitch):
    blocks, depth, _ = stage.shape

    def copy_of(i):
        some = pl.ds(i * 8, 8)
        return pltpu.make_async_copy(stage.at[some], out_ref.at[some], sems.at[i])

    @pl.loop(0, blocks // 8)
    def _(i):
        for e in range(8):
            at = pl.multiple_of(i * 8 * pitch, 8) + e * pitch
            stage[i * 8 + e] = wide[pl.ds(at, depth), :].astype(BF16)
        copy_of(i).start()

    @pl.loop(0, blocks // 8)
    def _(i):
        copy_of(i).wait()


def unpack_blocks(in_ref, wide, pitch):
    blocks, depth, _ = in_ref.shape

    @pl.loop(0, blocks // 8)
    def _(i):
        for e in range(8):
            at = pl.multiple_of(i * 8 * pitch, 8) + e * pitch
            wide[pl.ds(at, depth), :] = in_ref[i * 8 + e].astype(F32)


def choice_masks(routes_ref, experts, tokens):
    expert_id = lax.broadcasted_iota(jnp.int32, (experts, tokens), 0)
    first = routes_ref[0:1, :] == expert_id
    second = routes_ref[1:2, :] == expert_id
    either = first | second
    earlier = lax.broadcasted_iota(jnp.int32, (tokens, tokens), 0) < lax.broadcasted_iota(
        jnp.int32, (tokens, tokens), 1
    )
    rank = dot(jnp.where(either, 1.0, 0.0).astype(BF16), jnp.where(earlier, 1.0, 0.0).astype(BF16))
    return first, second, either, rank


def dispatch_body(slots, group_tokens, doc_count):
    def body(start_ref, x_hbm, g_hbm, routes_hbm, nums_hbm, lengths_hbm, send_ref, *scratches):
        wide, more, stage, x_ref, g_ref, routes_ref, nums_ref, lengths_ref, lsems, sems = scratches
        loads = [
            pltpu.make_async_copy(routes_hbm, routes_ref, lsems.at[0]),
            pltpu.make_async_copy(nums_hbm, nums_ref, lsems.at[1]),
            pltpu.make_async_copy(lengths_hbm, lengths_ref, lsems.at[2]),
            pltpu.make_async_copy(x_hbm, x_ref, lsems.at[3]),
            pltpu.make_async_copy(g_hbm, g_ref, lsems.at[4]),
        ]
        for load in loads:
            load.start()
        for load in loads[:3]:
            load.wait()
        experts = stage.shape[0]
        tokens, features = x_ref.shape
        tiles = features // LANES
        depth = slots * tiles
        pitch = depth + 4
        first, second, either, rank = choice_masks(routes_ref, experts, tokens)
        position = start_ref[0] + lax.broadcasted_iota(jnp.int32, (1, tokens), 1)
        own = jnp.zeros((1, tokens), jnp.int32)
        begin = jnp.int32(0)
        for j in range(doc_count):
            length = lengths_ref[0, j]
            own = jnp.where((position >= begin) & (position < begin + length), length, own)
            begin = begin + length
        weight = jnp.sqrt(jnp.float32(group_tokens) / (doc_count * own).astype(F32))
        factor = nums_ref[...].astype(F32) / 1024.0 * weight
        factors = jnp.where(first, factor[0:1, :], 0.0) + jnp.where(second, factor[1:2, :], 0.0)
        picks, scales = [], []
        for c in range(slots):
            chosen = jnp.where(either & (rank == float(c)), 1.0, 0.0)
            scales.append(jnp.sum(chosen * factors, axis=1, keepdims=True))
            picks.append(chosen.astype(BF16))
        pick = jnp.concatenate(picks, axis=0)
        scale = jnp.concatenate(scales, axis=0)
        chunk = 2 * LANES
        copies = []
        for side, (source, scratch) in enumerate(((x_ref, wide), (g_ref, more))):
            loads[3 + side].wait()
            for j in range(features // chunk):
                part = dot(pick, source[:, j * chunk : (j + 1) * chunk])
                if side == 1:
                    part = scale * part
                for c in range(slots):
                    for h in range(2):
                        scratch[pl.ds(c * tiles + 2 * j + h, experts, stride=pitch), :] = part[
                            c * experts : (c + 1) * experts, h * LANES : (h + 1) * LANES
                        ]
            at = pl.ds(side * depth, depth)
            for i in range(experts // 8):
                for e in range(i * 8, i * 8 + 8):
                    stage[e, at, :] = scratch[e * pitch : e * pitch + depth, :].astype(BF16)
                some = pl.ds(i * 8, 8)
                copies.append(
                    pltpu.make_async_copy(
                        stage.at[some, at], send_ref.at[some, at], sems.at[side, i]
                    )
                )
                copies[-1].start()
        for copy in copies:
            copy.wait()

    return body


def product_body(slots, places):
    def body(recv_ref, *refs):
        weight_refs, refs = refs[: len(places)], refs[len(places) :]
        left_ref, bdown_ref, right_ref, rows_out, s, gates, ups, lows_ref, weights, down = refs[:10]
        x, wide, more, sems, osems = refs[10:]
        peers = recv_ref.shape[0]
        features = x.shape[1]
        hidden = gates.shape[1]
        tiles = features // LANES
        depth = slots * tiles
        pitch = depth + 4
        narrow = tiles + 4
        copies = [[], [], []]
        for k, (ref, (m, at, size)) in enumerate(zip(weight_refs, places)):
            to = weights.at[m] if m < 2 else down
            copies[m].append(pltpu.make_async_copy(ref, to.at[pl.ds(at, size)], sems.at[k]))
        for copy in copies[0]:
            copy.start()
        for e in range(peers):
            wide[e * pitch : e * pitch + depth, :] = recv_ref[e, :depth, :].astype(F32)
        for j in range(tiles):
            for c in range(slots):
                x[c * peers : (c + 1) * peers, j * LANES : (j + 1) * LANES] = wide[
                    pl.ds(c * tiles + j, peers, stride=pitch), :
                ].astype(BF16)
        chunk = hidden // slots
        lows = dot(x[...], left_ref[...], NT)
        lows_ref[0] = lows[:, :16].astype(BF16)
        lows_ref[1] = lows[:, 16:].astype(BF16)
        for copy in copies[0]:
            copy.wait()
        for copy in copies[1]:
            copy.start()

        @pl.loop(0, slots)
        def _(c):
            cols = pl.ds(pl.multiple_of(c * chunk, chunk), chunk)
            gates[:, cols] = dot(x[...], weights[0, cols, :], NT) + SCALE * dot(
                lows_ref[0], right_ref[0, :, cols]
            )
            from_row = pl.multiple_of(depth + c * tiles, tiles)
            for e in range(peers):
                more[e * narrow : e * narrow + tiles, :] = recv_ref[e, pl.ds(from_row, tiles), :].astype(F32)
            for j in range(tiles):
                s[pl.ds(pl.multiple_of(c * peers, peers), peers), j * LANES : (j + 1) * LANES] = more[
                    pl.ds(j, peers, stride=narrow), :
                ].astype(BF16)

        for copy in copies[1]:
            copy.wait()
        out_copies = [
            pltpu.make_async_copy(x, rows_out.at[0], osems.at[0]),
            pltpu.make_async_copy(s, rows_out.at[1], osems.at[1]),
        ]
        for copy in copies[2] + out_copies:
            copy.start()
        for n in range(slots):
            cols = slice(n * chunk, (n + 1) * chunk)
            ups[:, cols] = dot(x[...], weights[1, cols, :], NT) + SCALE * dot(
                lows_ref[1], right_ref[1, :, cols]
            )
        lows_ref[2] = dot(s[...], bdown_ref[...], NT).astype(BF16)
        for copy in copies[2] + out_copies:
            copy.wait()

    return body


def expert_body(slots):
    def body(s, gates, ups, lows_ref, weights, near, *refs):
        far_refs, left_ref, right_ref, send_ref, acts_out, lows_out = refs[:2], *refs[2:7]
        wide, far, acts, all_lows, backs, stage, sems, ssems, osems = refs[7:]
        rows, features = s.shape
        hidden = gates.shape[1]
        peers = rows // slots
        tiles = features // LANES
        pitch = slots * tiles + 4
        chunk = 2 * LANES
        half = far_refs[0].shape[0]
        held = near.shape[0] // chunk * chunk
        keep = near.shape[0] - held
        copies = [pltpu.make_async_copy(near.at[pl.ds(held, keep)], far.at[pl.ds(0, keep)], sems.at[2])]
        for k in range(2):
            copies.append(
                pltpu.make_async_copy(far_refs[k], far.at[pl.ds(keep + k * half, half)], sems.at[k])
            )
        for copy in copies:
            copy.start()
        for n in range(hidden // chunk):
            cols = slice(n * chunk, (n + 1) * chunk)
            gate, up = gates[:, cols], ups[:, cols]
            if (n + 1) * chunk <= held:
                down = near[cols, :]
            else:
                for copy in copies:
                    copy.wait()
                down = far[...]
            back = dot(s[...], down, NT) + SCALE * dot(lows_ref[2], right_ref[2, :, cols])
            sigma = jax.nn.sigmoid(gate)
            active = gate * sigma
            acts[0, :, cols] = (active * up).astype(BF16)
            acts[1, :, cols] = (back * up * sigma * (1.0 + gate * (1.0 - sigma))).astype(BF16)
            acts[2, :, cols] = (back * active).astype(BF16)
        gate_back = dot(acts[1], right_ref[0], NT).astype(BF16)
        up_back = dot(acts[2], right_ref[1], NT).astype(BF16)
        all_lows[0:3] = lows_ref[...]
        all_lows[3] = gate_back
        all_lows[4] = up_back
        out_copies = [
            pltpu.make_async_copy(acts, acts_out, osems.at[0]),
            pltpu.make_async_copy(all_lows, lows_out, osems.at[1]),
        ]
        for copy in out_copies:
            copy.start()
        backs[:, :16] = gate_back
        backs[:, 16:] = up_back
        for j in range(features // chunk):
            cols = slice(j * chunk, (j + 1) * chunk)
            part = (
                dot(acts[1], weights[0, :, cols])
                + dot(acts[2], weights[1, :, cols])
                + SCALE * dot(backs[...], left_ref[:, cols])
            )
            for c in range(slots):
                for h in range(chunk // LANES):
                    wide[
                        pl.ds(c * tiles + j * (chunk // LANES) + h, peers, stride=pitch), :
                    ] = part[c * peers : (c + 1) * peers, h * LANES : (h + 1) * LANES]
        pack_blocks(wide, stage, send_ref, ssems, pitch)
        for copy in out_copies:
            copy.wait()

    return body


def adapter_body(slots, share, width):
    def body(me_ref, routes_ref, rows_ref, acts_ref, lows_ref, right_ref, *refs):
        shares = refs[:4]
        back_ref = refs[4]
        big, small = refs[5:]
        tokens = routes_ref.shape[1]
        experts = tokens
        down_low = dot(acts_ref[0], right_ref[2], NT).astype(BF16)
        big[0] = SCALE * dot(lows_ref[3], rows_ref[0], TN)
        big[1] = SCALE * dot(lows_ref[4], rows_ref[0], TN)
        big[2] = SCALE * dot(down_low, rows_ref[1], TN)
        small[0] = SCALE * dot(lows_ref[0], acts_ref[1], TN)
        small[1] = SCALE * dot(lows_ref[1], acts_ref[2], TN)
        small[2] = SCALE * dot(lows_ref[2], acts_ref[0], TN)
        for k in range(4):
            at = pl.multiple_of(((me_ref[0] + k) % 4) * width, width)
            for m in range(3):
                shares[k][m, :, 0:width] = big[m, :, pl.ds(at, width)]
                shares[k][m, :, width : width + share] = small[m, :, (k + 1) % 4 * share : ((k + 1) % 4 + 1) * share]
                shares[k][m, :, width + share :] = jnp.zeros((16, 256 - share), F32)
        _, _, either, rank = choice_masks(routes_ref, experts, tokens)
        for c in range(slots):
            back_ref[:, c * experts : (c + 1) * experts] = jnp.where(
                either & (rank == float(c)), 1.0, 0.0
            ).T.astype(BF16)

    return body


def total_body(share, width):
    def body(a_ref, b_ref, c_ref, d_ref, *outs):
        for m in range(3):
            total = a_ref[m] + b_ref[m] + c_ref[m] + d_ref[m]
            outs[m][...] = total[:, :width]
            outs[3 + m][...] = total[:, width : width + share]

    return body


def combine_body(slots):
    def body(back_ref, pick_ref, out_ref, wide, rows):
        experts = back_ref.shape[0]
        _, features = out_ref.shape
        tiles = features // LANES
        depth = slots * tiles

        unpack_blocks(back_ref, wide, depth + 4)
        for j in range(tiles):
            for c in range(slots):
                rows[c * experts : (c + 1) * experts, j * LANES : (j + 1) * LANES] = wide[
                    pl.ds(c * tiles + j, experts, stride=depth + 4), :
                ].astype(BF16)
        for j in range(0, features, 256):
            out_ref[:, j : j + 256] = dot(pick_ref[...], rows[:, j : j + 256]).astype(BF16)

    return body


def layer(
    hidden_in,
    out_grad,
    routes,
    gate_num,
    doc_lengths,
    w_gate,
    w_up,
    w_down,
    a_gate,
    b_gate,
    a_up,
    b_up,
    a_down,
    b_down,
):
    tokens, features = hidden_in.shape[1:]
    groups = lax.axis_size("expert")
    shards = lax.axis_size("dp")
    share = w_gate.shape[1]
    hidden = share * shards
    rank_dim = a_gate.shape[2]
    width = features // shards
    slots = min(tokens, max(2, 3 * tokens * routes.shape[2] // (2 * groups)))
    tiles = features // LANES
    depth = slots * tiles
    rows = slots * groups
    me = lax.axis_index("dp")
    routes_t = routes[0].T
    start = (lax.axis_index("expert") * tokens).astype(jnp.int32).reshape(1)
    x, g = hidden_in[0], out_grad[0]

    up_ring = [(i, (i + 1) % shards) for i in range(shards)]
    down_ring = [(i, (i - 1) % shards) for i in range(shards)]
    (send,) = call(
        dispatch_body(slots, tokens * groups, doc_lengths.shape[1]),
        (start, *in_hbm((x, g, routes_t, gate_num[0].T, doc_lengths))),
        [smem()] + [anyspace()] * 5,
        [((groups, 2 * depth, LANES), BF16, pltpu.HBM)],
        [anyspace()],
        [
            pltpu.VMEM((groups * (depth + 4), LANES), F32),
            pltpu.VMEM((groups * (depth + 4), LANES), F32),
            pltpu.VMEM((groups, 2 * depth, LANES), BF16),
            pltpu.VMEM((tokens, features), BF16),
            pltpu.VMEM((tokens, features), BF16),
            pltpu.VMEM(routes_t.shape, jnp.int32),
            pltpu.VMEM(routes_t.shape, jnp.int32),
            pltpu.SMEM(doc_lengths.shape, jnp.int32),
            pltpu.SemaphoreType.DMA((5,)),
            pltpu.SemaphoreType.DMA((2, groups // 8)),
        ],
        4 * rows * tokens * features,
        4 * rows * features,
        16,
    )
    own = (w_gate[0], w_up[0], w_down[0])
    recv = lax.all_to_all(send, "expert", split_axis=0, concat_axis=0, tiled=True)

    half = share // 2
    parts = []
    for w in own:
        behind = lax.ppermute(w, "dp", up_ring)
        ahead = lax.ppermute(w, "dp", down_ring)
        far = [lax.ppermute(behind[:half], "dp", up_ring), lax.ppermute(ahead[half:], "dp", down_ring)]
        parts.append((w, ahead, behind, *far))
    spots = ((share, share), (2 * share, share), (0, share), (3 * share, half), (3 * share + half, half))
    near = spots[:3]

    left = jnp.concatenate([a_gate[0].T, a_up[0].T], axis=0)
    right = jnp.stack([b_gate[0], b_up[0], a_down[0].T])
    right = lax.dynamic_slice_in_dim(
        jnp.concatenate([right, right], axis=2), (me + shards - 1) % shards * share, hidden, axis=2
    )
    row_blocks, s_rows, gates, ups, lows, both, near_down = call(
        product_body(
            slots,
            [(m, *spot) for m in range(2) for spot in spots] + [(2, *spot) for spot in near],
        ),
        (recv, *in_hbm((*parts[0], *parts[1], *parts[2][:3])), *in_vmem((left, b_down[0], right))),
        [vmem()] + [anyspace()] * 13 + [vmem()] * 3,
        [
            ((2, rows, features), BF16, pltpu.HBM),
            ((rows, features), BF16, pltpu.VMEM),
            ((rows, hidden), F32, pltpu.VMEM),
            ((rows, hidden), F32, pltpu.VMEM),
            ((3, rows, rank_dim), BF16, pltpu.VMEM),
            ((2, hidden, features), BF16, pltpu.VMEM),
            ((3 * share, features), BF16, pltpu.VMEM),
        ],
        [anyspace()] + [vmem()] * 6,
        [
            pltpu.VMEM((rows, features), BF16),
            pltpu.VMEM((groups * (depth + 4), LANES), F32),
            pltpu.VMEM((groups * (tiles + 4), LANES), F32),
            pltpu.SemaphoreType.DMA((13,)),
            pltpu.SemaphoreType.DMA((2,)),
        ],
        4 * rows * hidden * features,
        4 * hidden * features + 4 * rows * features,
        12,
    )
    send_back, acts, all_lows = call(
        expert_body(slots),
        (
            *in_vmem((s_rows, gates, ups, lows, both, near_down)),
            *in_hbm(parts[2][3:]),
            *in_vmem((left, right)),
        ),
        [vmem()] * 6 + [anyspace()] * 2 + [vmem()] * 2,
        [
            ((groups, depth, LANES), BF16, pltpu.HBM),
            ((3, rows, hidden), BF16, pltpu.HBM),
            ((5, rows, rank_dim), BF16, pltpu.HBM),
        ],
        [anyspace()] * 3,
        [
            pltpu.VMEM((groups * (depth + 4), LANES), F32),
            pltpu.VMEM((2 * LANES, features), BF16),
            pltpu.VMEM((3, rows, hidden), BF16),
            pltpu.VMEM((5, rows, rank_dim), BF16),
            pltpu.VMEM((rows, 2 * rank_dim), BF16),
            pltpu.VMEM((groups, depth, LANES), BF16),
            pltpu.SemaphoreType.DMA((3,)),
            pltpu.SemaphoreType.DMA((groups // 8,)),
            pltpu.SemaphoreType.DMA((2,)),
        ],
        6 * rows * hidden * features,
        2 * hidden * features + 2 * rows * features,
        18,
    )
    back = lax.all_to_all(send_back, "expert", split_axis=0, concat_axis=0, tiled=True)

    *shares, pick = call(
        adapter_body(slots, share, width),
        (
            me.astype(jnp.int32).reshape(1),
            *in_hbm((routes_t, row_blocks, acts, all_lows, right)),
        ),
        [smem()] + [vmem()] * 5,
        [((3, rank_dim, width + 256), F32, pltpu.HBM)] * 4 + [((tokens, rows), BF16, pltpu.VMEM)],
        [vmem()] * 5,
        [pltpu.VMEM((3, rank_dim, features), F32), pltpu.VMEM((3, rank_dim, hidden), F32)],
        12 * rows * features * rank_dim,
        4 * rows * features,
        12,
    )
    pieces = [shares[0]] + [
        lax.ppermute(shares[k], "dp", [(i, (i + k) % shards) for i in range(shards)])
        for k in range(1, shards)
    ]
    big_gate, big_up, big_down, small_gate, small_up, small_down = call(
        total_body(share, width),
        pieces,
        [vmem()] * 4,
        [((rank_dim, width), F32, pltpu.HBM)] * 3 + [((rank_dim, share), F32, pltpu.HBM)] * 3,
        [vmem()] * 6,
        [],
        9 * rank_dim * (width + share),
        60 * rank_dim * (width + share),
        4,
    )
    (input_grad,) = call(
        combine_body(slots),
        (back, pltpu.with_memory_space_constraint(pick, pltpu.VMEM)),
        [vmem()] * 2,
        [((tokens, features), BF16, pltpu.HBM)],
        [vmem()],
        [pltpu.VMEM((groups * (depth + 4), LANES), F32), pltpu.VMEM((rows, features), BF16)],
        2 * rows * tokens * features,
        2 * rows * features,
        12,
    )
    return (
        input_grad[None],
        big_gate.T[None],
        small_gate[None],
        big_up.T[None],
        small_up[None],
        small_down.T[None],
        big_down[None],
    )


def solution(mesh):
    return jax.shard_map(
        layer,
        mesh=mesh,
        in_specs=(
            P("dp", "expert", None),
            P("dp", "expert", None),
            P("dp", "expert", None),
            P("dp", "expert", None),
            P("dp", None),
            P("expert", "dp", None),
            P("expert", "dp", None),
            P("expert", "dp", None),
            P("expert", None, None),
            P("expert", None, None),
            P("expert", None, None),
            P("expert", None, None),
            P("expert", None, None),
            P("expert", None, None),
        ),
        out_specs=(
            P("dp", "expert", None),
            P("expert", "dp", None),
            P("expert", None, "dp"),
            P("expert", "dp", None),
            P("expert", None, "dp"),
            P("expert", "dp", None),
            P("expert", None, "dp"),
        ),
        check_vma=False,
    )
```
